32 devices in a mesh: tm: 16 (over z, y, x), pix: 2 (over core).
Axes of the slice: x: 2, y: 2, z: 4, core: 2. Of those that a mesh axis runs over, the one named last changes fastest.
Arguments:
- frames: float32 [2048, 16384], P('tm', 'pix'), may hold values from 0.04 to 830, as said below
- ref_weight: float32 [16384], P('pix'), may hold values from 0.02 to 15, as said below
Outputs:
- correlation: float32 [4, 16, 16384], P(None, None, 'pix')
The draws below stay inside these ranges and needn't reach their ends.
Inputs may be any that keep to these rules, and one draw needn't show every extreme that they name: `frames`: positive intensities. `ref_weight`: positive weights.
All inputs are finite; a program needn't handle non-finite values.
Results may differ from the reference program's by a relative error of at most 0.0001.
Values sent between devices are 32-bit elements; how exact they have to be, the bound alone decides.
No kernel may reach another device: no remote copies, remote signals or barrier semaphores. Data moves between devices by JAX's collectives and lax.ppermute only.
A program may use at most 64 MiB of HBM per device.

```python
import jax
import jax.numpy as jnp
from jax import lax

PD = 8192
LEVELS = 4
LAGS = 16
FRAMES = 2048
PIXELS = 16384


def draw_frames(key, part):
    first, second, third, fourth, fifth, sixth, seventh = jax.random.split(key, 7)
    top_value = 10.0
    noise = jax.random.uniform(third, (FRAMES, PIXELS), jnp.float32, 0.5, 1.5)
    top_log = jnp.log(top_value)
    shared_drift = jax.random.uniform(first, (FRAMES, 1), jnp.float32, 0.0, 0.3 * top_log)
    region_drift = jax.random.uniform(seventh, (FRAMES, 4), jnp.float32, 0.0, 0.7 * top_log)
    region_index = (jnp.arange(PIXELS, dtype=jnp.int32) * 4 // PIXELS).astype(jnp.int32)
    frame_scale = jnp.exp(shared_drift + jnp.take(region_drift, region_index, axis=1))
    pixel_scale = jnp.exp(jax.random.uniform(second, (1, PIXELS), jnp.float32, 0.0, top_log))
    beat_rate = jnp.exp(jax.random.uniform(fourth, (1, PIXELS), jnp.float32, jnp.log(0.005), jnp.log(0.3)))
    beat_phase = jax.random.uniform(fifth, (1, PIXELS), jnp.float32, -3.14159, 3.14159)
    beat_depth = jax.random.uniform(sixth, (1, PIXELS), jnp.float32, 0.2, 0.8)
    moments = jnp.arange(FRAMES, dtype=jnp.float32)[:, None]
    beating = 1.0 + beat_depth * jnp.cos(beat_rate * moments + beat_phase)
    return frame_scale * pixel_scale * beating * noise


def draw_ref_weight(key, part):
    rising = 1.0 + 2.0 * jnp.arange(PIXELS, dtype=jnp.float32) / PIXELS
    base = jnp.exp(jax.random.uniform(key, (PIXELS,), jnp.float32, jnp.log(0.02), jnp.log(5.0)))
    return base * rising


def setup_inputs(seed: int = 0) -> dict:
    key_list = jax.random.split(jax.random.key(seed), 3)
    frames = draw_frames(jax.random.fold_in(key_list[2], 71), 0)
    ref_weight = draw_ref_weight(jax.random.fold_in(key_list[2], 71), 0)
    return dict(frames=frames, ref_weight=ref_weight)


def coarsen(series):
    half_rows = series.shape[0] // 2
    return series.reshape(half_rows, 2, series.shape[1]).sum(axis=1) * 0.5


def reference(frames, ref_weight):
    ref_mean = jnp.sum(frames * ref_weight[None, :], axis=1) / jnp.sum(ref_weight)
    signal = frames + ref_mean[:, None]
    pixel_mean = jnp.sum(signal, axis=0) / FRAMES
    blocks = signal.reshape(FRAMES, PIXELS // PD, PD).transpose(1, 0, 2)

    def per_block(block):
        results = []
        current = block
        for level in range(LEVELS):
            row_count = current.shape[0]
            results.append(jnp.stack([jnp.sum(current[:row_count - lag_index] * current[lag_index:], axis=0) for lag_index in range(1, LAGS + 1)]))
            if level < LEVELS - 1:
                current = coarsen(current)
        return jnp.stack(results)

    totals = lax.map(per_block, blocks).transpose(1, 2, 0, 3).reshape(LEVELS, LAGS, PIXELS)
    pair_counts = jnp.asarray([[(FRAMES >> level) - lag_index for lag_index in range(1, LAGS + 1)] for level in range(LEVELS)], jnp.float32)
    return totals / (pair_counts[:, :, None] * (pixel_mean * pixel_mean)[None, None, :])
```

```python
import functools

import jax
import jax.numpy as jnp
from jax import lax
from jax.experimental import pallas as pl
from jax.experimental.pallas import tpu as pltpu
from jax.sharding import PartitionSpec as P

LEVELS = 4
LAGS = 16
SUB, LANE = 8, 128
GROUP = SUB * LANE
VMEM_LIMIT = 48 * 1024 * 1024


def stack_tile(x_ref, tall_ref, row_tiles):
    for i in range(row_tiles):
        for c in range(SUB):
            tall_ref[pl.ds(i * SUB * SUB + c, SUB, stride=SUB), :] = x_ref[
                i * SUB : (i + 1) * SUB, c * LANE : (c + 1) * LANE
            ]


def tile(ref, row):
    return ref[row * SUB : (row + 1) * SUB, :]


def edge_kernel(x_ref, w_ref, sums_ref, edge_ref, tall_ref, acc_ref):
    rows = x_ref.shape[0]

    @pl.when(pl.program_id(0) == 0)
    def _():
        acc_ref[...] = jnp.zeros_like(acc_ref)

    for c in range(SUB):
        weight = jnp.broadcast_to(w_ref[:, c * LANE : (c + 1) * LANE], (SUB, LANE))
        acc_ref[rows : rows + SUB, :] += weight
        for i in range(rows // SUB):
            part = slice(i * SUB, (i + 1) * SUB)
            acc_ref[part, :] += x_ref[part, c * LANE : (c + 1) * LANE] * weight
    stack_tile(x_ref, tall_ref, rows // SUB)
    edge_ref[0, : LAGS * SUB, :] = tall_ref[: LAGS * SUB, :]
    half = LAGS // 2
    for level in range(1, LEVELS):
        span = 1 << level
        for j in range(half):
            group = [tile(tall_ref, (half + j) * span + s) for s in range(span)]
            while len(group) > 1:
                group = [(a + b) * 0.5 for a, b in zip(group[::2], group[1::2])]
            row = LAGS + (level - 1) * half + j
            edge_ref[0, row * SUB : (row + 1) * SUB, :] = group[0]

    @pl.when(pl.program_id(0) == pl.num_programs(0) - 1)
    def _():
        sums_ref[...] = jnp.sum(acc_ref[...], axis=1, keepdims=True)


def lag_step(old, new, totals):
    out = list(totals)
    for k in range(1, LAGS + 1):
        terms = []
        for i in range(LAGS):
            if i + k < LAGS:
                terms.append(old[i] * old[i + k])
            elif new is not None:
                terms.append(old[i] * new[i + k - LAGS])
        if terms:
            total = terms[0]
            for term in terms[1:]:
                total = total + term
            out[k - 1] = out[k - 1] + total
    return out


def inner_kernel(mean_ref, x_ref, totals_ref, last_ref, sum_ref, series_ref):
    rows = x_ref.shape[0]
    stack_tile(x_ref, series_ref, rows // SUB)

    def add_mean(t, total):
        at = pl.ds(pl.multiple_of(t * SUB, SUB), SUB)
        value = series_ref[at, :] + mean_ref[t]
        series_ref[at, :] = value
        return total + value

    sum_ref[0] = lax.fori_loop(
        0, rows, add_mean, jnp.zeros((SUB, LANE), jnp.float32), unroll=8
    )
    zero = jnp.zeros((SUB, LANE), jnp.float32)
    for level in range(LEVELS):
        count = rows >> level
        chunks = count // LAGS

        def load(chunk):
            start = pl.multiple_of(chunk * LAGS * SUB, SUB)
            block = series_ref[pl.ds(start, LAGS * SUB), :]
            return [block[i * SUB : (i + 1) * SUB] for i in range(LAGS)]

        def body(chunk, totals):
            return tuple(lag_step(load(chunk), load(chunk + 1), totals))

        totals = tuple([zero] * LAGS)
        if chunks > 1:
            totals = lax.fori_loop(0, chunks - 1, body, totals)
        old = load(chunks - 1)
        totals = lag_step(old, None, totals)
        for i in range(LAGS):
            row = level * LAGS + i
            totals_ref[0, row * SUB : (row + 1) * SUB, :] = totals[i]
            last_ref[0, row * SUB : (row + 1) * SUB, :] = old[i]
        if level < LEVELS - 1:
            def coarsen(i, carry):
                start = pl.multiple_of(i * 2 * SUB, SUB)
                pair = series_ref[pl.ds(start, 2 * SUB), :]
                series_ref[pl.ds(pl.multiple_of(i * SUB, SUB), SUB), :] = (
                    pair[:SUB] + pair[SUB:]
                ) * 0.5
                return carry

            lax.fori_loop(0, count // 2, coarsen, 0, unroll=4)


def border_kernel(mean_ref, edge_ref, last_ref, totals_ref, out_ref):
    half = LAGS // 2
    means = [mean_ref[t] for t in range(LAGS << (LEVELS - 1))]
    new = None
    for level in range(LEVELS):
        if level == 0:
            new = [
                edge_ref[0, j * SUB : (j + 1) * SUB, :] + means[j] for j in range(LAGS)
            ]
        else:
            means = [(a + b) * 0.5 for a, b in zip(means[::2], means[1::2])]
            first = [(a + b) * 0.5 for a, b in zip(new[::2], new[1::2])]
            second = []
            for j in range(half):
                row = LAGS + (level - 1) * half + j
                second.append(edge_ref[0, row * SUB : (row + 1) * SUB, :] + means[half + j])
            new = first + second
        old = [
            last_ref[0, (level * LAGS + i) * SUB : (level * LAGS + i + 1) * SUB, :]
            for i in range(LAGS)
        ]
        for k in range(1, LAGS + 1):
            at = slice((level * LAGS + k - 1) * SUB, (level * LAGS + k) * SUB)
            total = totals_ref[0, at, :]
            for i in range(LAGS - k, LAGS):
                total = total + old[i] * new[i + k - LAGS]
            out_ref[0, at, :] = total


def finish_kernel(total_frames, totals_ref, sum_ref, out_ref):
    for c in range(SUB):
        mean = sum_ref[0, c : c + 1, :] / total_frames
        square = jnp.broadcast_to(mean * mean, (SUB, LANE))
        for level in range(LEVELS):
            for i in range(LAGS // SUB):
                lag = lax.broadcasted_iota(jnp.int32, (SUB, LANE), 0) + (i * SUB + 1)
                count = ((total_frames >> level) - lag).astype(jnp.float32)
                row = level * LAGS + i * SUB
                total = totals_ref[0, pl.ds(row * SUB + c, SUB, stride=SUB), :]
                out_ref[level, i * SUB : (i + 1) * SUB, c * LANE : (c + 1) * LANE] = (
                    total / (count * square)
                )


def params():
    return pltpu.CompilerParams(vmem_limit_bytes=VMEM_LIMIT)


def f32(*shape):
    return jax.ShapeDtypeStruct(shape, jnp.float32)


def by_group(rows):
    return pl.BlockSpec((1, rows * SUB, LANE), lambda g: (g, 0, 0))


SMEM = pl.BlockSpec(memory_space=pltpu.SMEM)
ROWS = LEVELS * LAGS
EDGE_ROWS = LAGS + (LEVELS - 1) * (LAGS // 2)


def swap(block, mask):
    size = lax.axis_size("tm")
    return lax.ppermute(block, "tm", [(i, i ^ mask) for i in range(size)])


def sum_parts(parts, orders):
    me = lax.axis_index("tm")
    count = len(parts)
    steps = len(orders[0])
    cur = [p[0] for p in parts]
    sums = [p[1] for p in parts]
    for s in range(steps):
        kept, sent = [], []
        for p in range(count):
            half = cur[p].shape[1] // 2
            upper = (me & orders[p][s]) != 0
            low, high = cur[p][:, :half], cur[p][:, half:]
            kept.append(jnp.where(upper, high, low))
            sent.append(
                jnp.concatenate([jnp.where(upper, low, high), sums[p]], axis=1)
            )
        for p in range(count):
            half = kept[p].shape[1]
            got = swap(sent[p], orders[p][s])
            cur[p] = kept[p] + got[:, :half]
            sums[p] = sums[p] + got[:, half:]
    for s in reversed(range(steps)):
        for p in range(count):
            upper = (me & orders[p][s]) != 0
            got = swap(cur[p], orders[p][s])
            cur[p] = jnp.concatenate(
                [jnp.where(upper, got, cur[p]), jnp.where(upper, cur[p], got)], axis=1
            )
    return cur, sums


def on_device(frames, ref_weight):
    rows, pixels = frames.shape
    groups = pixels // GROUP
    size = lax.axis_size("tm")
    total_frames = rows * size
    block = pl.BlockSpec((rows, GROUP), lambda g: (0, g))
    sums, edge = pl.pallas_call(
        edge_kernel,
        grid=(groups,),
        in_specs=[block, pl.BlockSpec((1, GROUP), lambda g: (0, g))],
        out_specs=[pl.BlockSpec((rows + SUB, 1), lambda g: (0, 0)), by_group(EDGE_ROWS)],
        out_shape=[f32(rows + SUB, 1), f32(groups, EDGE_ROWS * SUB, LANE)],
        scratch_shapes=[
            pltpu.VMEM((rows * SUB, LANE), jnp.float32),
            pltpu.VMEM((rows + SUB, LANE), jnp.float32),
        ],
        compiler_params=params(),
        name="edges",
    )(frames, ref_weight.reshape(1, pixels))
    back = [(i, i - 1) for i in range(1, size)]
    next_edge = lax.ppermute(edge, "tm", back)
    sums = lax.psum(sums[:, 0], "pix")
    mean = sums[:rows] / sums[rows]
    next_mean = lax.ppermute(mean, "tm", back)
    totals, last, pixel_sum = pl.pallas_call(
        inner_kernel,
        grid=(groups,),
        in_specs=[SMEM, block],
        out_specs=[by_group(ROWS), by_group(ROWS), by_group(1)],
        out_shape=[
            f32(groups, ROWS * SUB, LANE),
            f32(groups, ROWS * SUB, LANE),
            f32(groups, SUB, LANE),
        ],
        scratch_shapes=[pltpu.VMEM((rows * SUB, LANE), jnp.float32)],
        compiler_params=params(),
        name="inner",
    )(mean, frames)
    totals = pl.pallas_call(
        border_kernel,
        grid=(groups,),
        in_specs=[SMEM, by_group(EDGE_ROWS), by_group(ROWS), by_group(ROWS)],
        out_specs=by_group(ROWS),
        out_shape=f32(groups, ROWS * SUB, LANE),
        compiler_params=params(),
        name="border",
    )(next_mean, next_edge, last, totals)
    bits = [1 << b for b in range(size.bit_length() - 1)]
    turn = bits[:-1]
    orders = [turn + bits[-1:], turn[1:] + turn[:1] + bits[-1:]]
    cut = groups // 2
    parts = [(totals[:cut], pixel_sum[:cut]), (totals[cut:], pixel_sum[cut:])]
    cur, sums = sum_parts(parts, orders)
    totals = jnp.concatenate(cur, axis=0)
    pixel_sum = jnp.concatenate(sums, axis=0)
    return pl.pallas_call(
        functools.partial(finish_kernel, total_frames),
        grid=(groups,),
        in_specs=[by_group(ROWS), by_group(1)],
        out_specs=pl.BlockSpec((LEVELS, LAGS, GROUP), lambda g: (0, 0, g)),
        out_shape=f32(LEVELS, LAGS, pixels),
        compiler_params=params(),
        name="finish",
    )(totals, pixel_sum)


def solution(mesh):
    return jax.shard_map(
        on_device,
        mesh=mesh,
        in_specs=(P("tm", "pix"), P("pix")),
        out_specs=P(None, None, "pix"),
        check_vma=False,
    )
```

```python
import functools

import jax
import jax.numpy as jnp
from jax import lax
from jax.experimental import pallas as pl
from jax.experimental.pallas import tpu as pltpu
from jax.sharding import PartitionSpec as P

LEVELS = 4
LAGS = 16
SUB, LANE = 8, 128
GROUP = SUB * LANE
VMEM_LIMIT = 16 * 1024 * 1024


def stack_tile(x_ref, tall_ref, row_tiles):
    for i in range(row_tiles):
        for c in range(SUB):
            tall_ref[pl.ds(i * SUB * SUB + c, SUB, stride=SUB), :] = x_ref[
                i * SUB : (i + 1) * SUB, c * LANE : (c + 1) * LANE
            ]


def tile(ref, row):
    return ref[row * SUB : (row + 1) * SUB, :]


def edge_kernel(x_hbm, w_hbm, sums_ref, edge_ref, x_ref, w_ref, tall_ref, acc_ref, sem, w_sem):
    groups, rows, _ = x_ref.shape
    half = LAGS // 2

    def fetch(g):
        at = pl.ds(pl.multiple_of(g * GROUP, GROUP), GROUP)
        return pltpu.make_async_copy(x_hbm.at[:, at], x_ref.at[g], sem.at[g])

    weights = pltpu.make_async_copy(w_hbm, w_ref, w_sem)
    weights.start()
    for g in range(groups):
        fetch(g).start()
    acc_ref[...] = jnp.zeros_like(acc_ref)
    weights.wait()

    def one_group(g, carry):
        fetch(g).wait()
        for c in range(SUB):
            at = pl.ds(pl.multiple_of(g * GROUP + c * LANE, LANE), LANE)
            weight = jnp.broadcast_to(w_ref[:, at], (SUB, LANE))
            acc_ref[rows : rows + SUB, :] += weight
            for i in range(rows // SUB):
                part = slice(i * SUB, (i + 1) * SUB)
                value = x_ref[g, part, c * LANE : (c + 1) * LANE]
                acc_ref[part, :] += value * weight
                tall_ref[pl.ds(i * SUB * SUB + c, SUB, stride=SUB), :] = value
        edge_ref[g, : LAGS * SUB, :] = tall_ref[: LAGS * SUB, :]
        for level in range(1, LEVELS):
            span = 1 << level
            for j in range(half):
                group = [tile(tall_ref, (half + j) * span + s) for s in range(span)]
                while len(group) > 1:
                    group = [(a + b) * 0.5 for a, b in zip(group[::2], group[1::2])]
                row = LAGS + (level - 1) * half + j
                edge_ref[g, row * SUB : (row + 1) * SUB, :] = group[0]
        return carry

    lax.fori_loop(0, groups, one_group, 0)
    sums_ref[...] = jnp.sum(acc_ref[...], axis=1, keepdims=True)


def lag_step(old, new, totals):
    out = list(totals)
    for k in range(1, LAGS + 1):
        terms = []
        for i in range(LAGS):
            if i + k < LAGS:
                terms.append(old[i] * old[i + k])
            elif new is not None:
                terms.append(old[i] * new[i + k - LAGS])
        if terms:
            total = terms[0]
            for term in terms[1:]:
                total = total + term
            out[k - 1] = out[k - 1] + total
    return out


def inner_kernel(mean_ref, x_ref, totals_ref, last_ref, sum_ref, series_ref):
    rows = x_ref.shape[0]
    stack_tile(x_ref, series_ref, rows // SUB)

    def add_mean(t, total):
        at = pl.ds(pl.multiple_of(t * SUB, SUB), SUB)
        value = series_ref[at, :] + mean_ref[t]
        series_ref[at, :] = value
        return total + value

    sum_ref[0] = lax.fori_loop(
        0, rows, add_mean, jnp.zeros((SUB, LANE), jnp.float32), unroll=8
    )
    zero = jnp.zeros((SUB, LANE), jnp.float32)
    for level in range(LEVELS):
        count = rows >> level
        chunks = count // LAGS

        def load(chunk):
            start = pl.multiple_of(chunk * LAGS * SUB, SUB)
            block = series_ref[pl.ds(start, LAGS * SUB), :]
            return [block[i * SUB : (i + 1) * SUB] for i in range(LAGS)]

        def body(chunk, totals):
            return tuple(lag_step(load(chunk), load(chunk + 1), totals))

        totals = tuple([zero] * LAGS)
        if chunks > 1:
            totals = lax.fori_loop(0, chunks - 1, body, totals)
        old = load(chunks - 1)
        totals = lag_step(old, None, totals)
        for i in range(LAGS):
            row = level * LAGS + i
            totals_ref[0, row * SUB : (row + 1) * SUB, :] = totals[i]
            last_ref[0, row * SUB : (row + 1) * SUB, :] = old[i]
        if level < LEVELS - 1:
            def coarsen(i, carry):
                start = pl.multiple_of(i * 2 * SUB, SUB)
                pair = series_ref[pl.ds(start, 2 * SUB), :]
                series_ref[pl.ds(pl.multiple_of(i * SUB, SUB), SUB), :] = (
                    pair[:SUB] + pair[SUB:]
                ) * 0.5
                return carry

            lax.fori_loop(0, count // 2, coarsen, 0, unroll=4)


def border_kernel(first, mean_ref, side_ref, edge_ref, last_ref, totals_ref,
                  sum_ref, kept_ref, sent_ref, level_mean_ref):
    half = LAGS // 2
    split = LEVELS // 2
    side = side_ref[0]
    groups = kept_ref.shape[0]
    for j in range(LAGS):
        level_mean_ref[j] = mean_ref[j]
    for level in range(1, LEVELS):
        span = 1 << level
        for j in range(half):
            group = [mean_ref[(half + j) * span + s] for s in range(span)]
            while len(group) > 1:
                group = [(a + b) * 0.5 for a, b in zip(group[::2], group[1::2])]
            level_mean_ref[LAGS + (level - 1) * half + j] = group[0]

    def one_group(slot, carry):
        g = slot + first
        sent_ref[slot, ROWS // 2 * SUB :, :] = sum_ref[slot]
        new = [
            edge_ref[g, j * SUB : (j + 1) * SUB, :] + level_mean_ref[j]
            for j in range(LAGS)
        ]
        for level in range(LEVELS):
            if level > 0:
                fresh = [(a + b) * 0.5 for a, b in zip(new[::2], new[1::2])]
                for j in range(half):
                    row = LAGS + (level - 1) * half + j
                    fresh.append(
                        edge_ref[g, row * SUB : (row + 1) * SUB, :] + level_mean_ref[row]
                    )
                new = fresh
            base = level * LAGS
            old = [
                last_ref[slot, (base + i) * SUB : (base + i + 1) * SUB, :]
                for i in range(LAGS)
            ]
            totals = []
            for k in range(1, LAGS + 1):
                row = base + k - 1
                total = totals_ref[slot, row * SUB : (row + 1) * SUB, :]
                for i in range(LAGS - k, LAGS):
                    total = total + old[i] * new[i + k - LAGS]
                totals.append(total)
            upper, base = level // split, (level % split) * LAGS

            def put(ref, totals=totals, base=base):
                for i, total in enumerate(totals):
                    ref[slot, (base + i) * SUB : (base + i + 1) * SUB, :] = total

            pl.when(side == upper)(functools.partial(put, kept_ref))
            pl.when(side != upper)(functools.partial(put, sent_ref))
        return carry

    lax.fori_loop(0, groups, one_group, 0)


def finish_kernel(total_frames, side_ref, mine_ref, got_ref, sum_ref, *refs):
    out_ref = refs[-1]
    split = LEVELS // 2
    g = pl.program_id(0)
    side = side_ref[0]
    for c in range(SUB):
        mean = sum_ref[g, c : c + 1, :] / total_frames
        square = jnp.broadcast_to(mean * mean, (SUB, LANE))
        for level in range(LEVELS):
            own = side == level // split
            for i in range(LAGS // SUB):
                lag = lax.broadcasted_iota(jnp.int32, (SUB, LANE), 0) + (i * SUB + 1)
                count = ((total_frames >> level) - lag).astype(jnp.float32)
                row = (level % split) * LAGS + i * SUB
                at = pl.ds(row * SUB + c, SUB, stride=SUB)
                total = jnp.where(own, mine_ref[g, at, :], got_ref[g, at, :])
                out_ref[level, i * SUB : (i + 1) * SUB, c * LANE : (c + 1) * LANE] = (
                    total / (count * square)
                )


ROWS = LEVELS * LAGS
EDGE_ROWS = LAGS + (LEVELS - 1) * (LAGS // 2)
SMEM = pl.BlockSpec(memory_space=pltpu.SMEM)
VMEM = pl.BlockSpec(memory_space=pltpu.VMEM)


def params():
    return pltpu.CompilerParams(vmem_limit_bytes=VMEM_LIMIT)


def in_hbm(value):
    return pltpu.with_memory_space_constraint(value, pltpu.HBM)


def f32(*shape):
    return jax.ShapeDtypeStruct(shape, jnp.float32)


def by_group(rows):
    return pl.BlockSpec((1, rows * SUB, LANE), lambda g: (g, 0, 0))


def swap(block, mask):
    size = lax.axis_size("tm")
    return lax.ppermute(block, "tm", [(i, i ^ mask) for i in range(size)])


class Part:
    def __init__(self, order, uppers, kept, sent):
        self.order = order
        self.uppers = uppers
        self.step = 0
        self.kept, self.sent = kept, sent
        self.sums = sent[:, kept.shape[1] :]

    def send(self):
        mask = self.order[self.step]
        last = self.step == len(self.order) - 1
        if self.step > 0:
            if last:
                self.kept, self.sent = self.cur, self.cur
            else:
                half = self.cur.shape[1] // 2
                upper = self.uppers[mask]
                low, high = self.cur[:, :half], self.cur[:, half:]
                self.kept = jnp.where(upper, high, low)
                self.sent = jnp.where(upper, low, high)
            self.sent = jnp.concatenate([self.sent, self.sums], axis=1)
        self.got = swap(self.sent, mask)

    def receive(self):
        rows = self.kept.shape[1]
        self.cur = self.kept + self.got[:, :rows]
        self.sums = self.sums + self.got[:, rows:]
        self.step += 1

    def send_back(self, step):
        self.got = swap(self.cur, self.order[step])

    def receive_back(self, step):
        upper = self.uppers[self.order[step]]
        low = jnp.where(upper, self.got, self.cur)
        high = jnp.where(upper, self.cur, self.got)
        self.cur = jnp.concatenate([low, high], axis=1)


def on_device(frames, ref_weight):
    rows, pixels = frames.shape
    groups = pixels // GROUP
    size = lax.axis_size("tm")
    total_frames = rows * size
    bits = [1 << b for b in range(size.bit_length() - 1)]
    me = lax.axis_index("tm")
    uppers = {bit: (me & bit) != 0 for bit in bits}
    sides = {bit: uppers[bit].astype(jnp.int32).reshape(1) for bit in bits[:2]}
    ref_weight, uppers, sides = lax.optimization_barrier((ref_weight, uppers, sides))
    stored = in_hbm(frames)
    back = [(i, i - 1) for i in range(1, size)]
    sums, edge = pl.pallas_call(
        edge_kernel,
        in_specs=[pl.BlockSpec(memory_space=pl.ANY)] * 2,
        out_specs=[VMEM, VMEM],
        out_shape=[f32(rows + SUB, 1), f32(groups, EDGE_ROWS * SUB, LANE)],
        scratch_shapes=[
            pltpu.VMEM((groups, rows, GROUP), jnp.float32),
            pltpu.VMEM((1, pixels), jnp.float32),
            pltpu.VMEM((rows * SUB, LANE), jnp.float32),
            pltpu.VMEM((rows + SUB, LANE), jnp.float32),
            pltpu.SemaphoreType.DMA((groups,)),
            pltpu.SemaphoreType.DMA,
        ],
        compiler_params=params(),
        name="edges",
    )(stored, in_hbm(ref_weight.reshape(1, pixels)))
    next_edge = lax.ppermute(edge, "tm", back)
    sums = lax.psum(sums[:, 0], "pix")
    mean = sums[:rows] / sums[rows]
    next_mean = lax.ppermute(mean, "tm", back)
    orders = [
        bits[:1] + bits[2:3] + bits[1:2] + bits[3:],
        bits[1:2] + bits[:1] + bits[2:],
    ]
    count = groups // 2
    inner = []
    for p in range(len(orders)):
        sums = pl.pallas_call(
            inner_kernel,
            grid=(count,),
            in_specs=[
                SMEM,
                pl.BlockSpec((rows, GROUP), lambda g, first=p * count: (0, g + first)),
            ],
            out_specs=[by_group(ROWS), by_group(ROWS), by_group(1)],
            out_shape=[
                f32(count, ROWS * SUB, LANE),
                f32(count, ROWS * SUB, LANE),
                f32(count, SUB, LANE),
            ],
            scratch_shapes=[pltpu.VMEM((rows * SUB, LANE), jnp.float32)],
            compiler_params=params(),
            name=f"inner_{p}",
        )(mean, stored)
        inner.append(sums)
    next_edge, inner = lax.optimization_barrier((next_edge, inner))
    parts = []
    for p, order in enumerate(orders):
        totals, last, pixel_sum = inner[p]
        kept, sent = pl.pallas_call(
            functools.partial(border_kernel, p * count),
            in_specs=[SMEM, SMEM] + [VMEM] * 4,
            out_specs=[VMEM, VMEM],
            out_shape=[
                f32(count, ROWS // 2 * SUB, LANE),
                f32(count, (ROWS // 2 + 1) * SUB, LANE),
            ],
            scratch_shapes=[
                pltpu.SMEM((LAGS + EDGE_ROWS,), jnp.float32),
            ],
            compiler_params=params(),
            name=f"border_{p}",
        )(
            next_mean,
            sides[order[0]],
            next_edge,
            last,
            totals,
            pixel_sum,
        )
        parts.append(Part(order, uppers, kept, sent))
    steps = len(bits)
    for part in parts:
        part.send()
    for step in range(1, steps + 1):
        for part in parts:
            part.receive()
            if step < steps:
                part.send()
            else:
                part.send_back(steps - 2)
    for step in reversed(range(1, steps - 1)):
        for part in parts:
            part.receive_back(step)
            part.send_back(step - 1)
    out = None
    for p, part in enumerate(parts):
        first = p * count
        held = [] if out is None else [out]
        out = pl.pallas_call(
            functools.partial(finish_kernel, total_frames),
            grid=(count,),
            in_specs=[SMEM, VMEM, VMEM, VMEM]
            + [pl.BlockSpec(memory_space=pl.ANY)] * len(held),
            out_specs=pl.BlockSpec(
                (LEVELS, LAGS, GROUP), lambda g, first=first: (0, 0, g + first)
            ),
            out_shape=f32(LEVELS, LAGS, pixels),
            input_output_aliases={4: 0} if held else {},
            compiler_params=params(),
            name=f"finish_{p}",
        )(sides[part.order[0]], part.cur, part.got, part.sums, *held)
    return out


def solution(mesh):
    return jax.shard_map(
        on_device,
        mesh=mesh,
        in_specs=(P("tm", "pix"), P("pix")),
        out_specs=P(None, None, "pix"),
        check_vma=False,
    )
```

```python
import functools

import jax
import jax.numpy as jnp
from jax import lax
from jax.experimental import pallas as pl
from jax.experimental.pallas import tpu as pltpu
from jax.sharding import PartitionSpec as P

LEVELS = 4
LAGS = 16
SUB, LANE = 8, 128
GROUP = SUB * LANE
VMEM_LIMIT = 16 * 1024 * 1024


def tile(ref, row):
    return ref[row * SUB : (row + 1) * SUB, :]


def edge_kernel(spans, x_hbm, w_hbm, sums_ref, *refs):
    edge_refs, refs = refs[: len(spans)], refs[len(spans) :]
    x_ref, w_ref, tall_ref, acc_ref, sem, w_sem = refs
    groups, rows, _ = x_ref.shape
    half = LAGS // 2

    def fetch(g):
        at = pl.ds(pl.multiple_of(g * GROUP, GROUP), GROUP)
        return pltpu.make_async_copy(x_hbm.at[:, at], x_ref.at[g], sem.at[g])

    weights = pltpu.make_async_copy(w_hbm, w_ref, w_sem)
    weights.start()
    for g in range(groups):
        fetch(g).start()
    acc_ref[...] = jnp.zeros_like(acc_ref)
    weights.wait()

    def one_group(first, edge_ref, slot, carry):
        g = slot + first
        fetch(g).wait()
        for c in range(SUB):
            at = pl.ds(pl.multiple_of(g * GROUP + c * LANE, LANE), LANE)
            weight = jnp.broadcast_to(w_ref[:, at], (SUB, LANE))
            acc_ref[rows : rows + SUB, :] += weight
            for i in range(rows // SUB):
                part = slice(i * SUB, (i + 1) * SUB)
                value = x_ref[g, part, c * LANE : (c + 1) * LANE]
                acc_ref[part, :] += value * weight
                tall_ref[pl.ds(i * SUB * SUB + c, SUB, stride=SUB), :] = value
        edge_ref[slot, : LAGS * SUB, :] = tall_ref[: LAGS * SUB, :]
        for level in range(1, LEVELS):
            span = 1 << level
            for j in range(half):
                group = [tile(tall_ref, (half + j) * span + s) for s in range(span)]
                while len(group) > 1:
                    group = [(a + b) * 0.5 for a, b in zip(group[::2], group[1::2])]
                row = LAGS + (level - 1) * half + j
                edge_ref[slot, row * SUB : (row + 1) * SUB, :] = group[0]
        return carry

    for (first, count), edge_ref in zip(spans, edge_refs):
        lax.fori_loop(0, count, functools.partial(one_group, first, edge_ref), 0)
    sums_ref[...] = jnp.sum(acc_ref[...], axis=1, keepdims=True)


def lag_step(read, near, far, totals):
    window = [read(i) for i in range(LAGS)]
    out = list(totals)
    for i in range(near):
        for k in range(1, LAGS + 1):
            if i + k < far:
                if i + k == len(window):
                    window.append(read(i + k))
                out[k - 1] = out[k - 1] + window[i] * window[i + k]
    return out


def inner_kernel(mean_ref, x_ref, totals_ref, last_ref, sum_ref, series_ref, wide_ref):
    rows = x_ref.shape[0]

    @pl.when(pl.program_id(0) == 0)
    def _():
        for t in range(rows):
            wide_ref[t : t + 1, :] = jnp.full((1, LANE), mean_ref[t], jnp.float32)

    for c in range(SUB):
        total = None
        for i in range(rows // SUB):
            part = slice(i * SUB, (i + 1) * SUB)
            value = x_ref[part, c * LANE : (c + 1) * LANE] + wide_ref[part, :]
            series_ref[pl.ds(i * SUB * SUB + c, SUB, stride=SUB), :] = value
            total = value if total is None else total + value
        sum_ref[0, c : c + 1, :] = jnp.sum(total, axis=0, keepdims=True)
    zero = jnp.zeros((SUB, LANE), jnp.float32)
    for level in range(LEVELS):
        count = rows >> level
        chunks = count // LAGS

        def reader(chunk):
            start = chunk * (LAGS * SUB)

            def read(i):
                return series_ref[pl.ds(pl.multiple_of(start + i * SUB, SUB), SUB), :]

            return read

        def body(chunk, totals):
            return tuple(lag_step(reader(chunk), LAGS, 2 * LAGS, totals))

        totals = tuple([zero] * LAGS)
        if chunks > 1:
            totals = lax.fori_loop(0, chunks - 1, body, totals)
        read = reader(chunks - 1)
        totals = lag_step(read, LAGS, LAGS, totals)
        old = [read(i) for i in range(LAGS)]
        for i in range(LAGS):
            row = level * LAGS + i
            totals_ref[0, row * SUB : (row + 1) * SUB, :] = totals[i]
            last_ref[0, row * SUB : (row + 1) * SUB, :] = old[i]
        if level < LEVELS - 1:
            for i in range(count // 2):
                pair = tile(series_ref, 2 * i) + tile(series_ref, 2 * i + 1)
                series_ref[i * SUB : (i + 1) * SUB, :] = pair * 0.5


def border_kernel(offset, mean_ref, side_ref, edge_ref, last_ref, totals_ref,
                  sum_ref, kept_ref, sent_ref, level_mean_ref):
    half = LAGS // 2
    split = LEVELS // 2
    side = side_ref[0]
    groups = kept_ref.shape[0]
    for j in range(LAGS):
        level_mean_ref[j] = mean_ref[j]
    for level in range(1, LEVELS):
        span = 1 << level
        for j in range(half):
            group = [mean_ref[(half + j) * span + s] for s in range(span)]
            while len(group) > 1:
                group = [(a + b) * 0.5 for a, b in zip(group[::2], group[1::2])]
            level_mean_ref[LAGS + (level - 1) * half + j] = group[0]

    def one_group(slot, carry):
        sent_ref[slot, ROWS // 2 * SUB :, :] = sum_ref[slot]
        new = [
            edge_ref[slot + offset, j * SUB : (j + 1) * SUB, :] + level_mean_ref[j]
            for j in range(LAGS)
        ]
        for level in range(LEVELS):
            if level > 0:
                fresh = [(a + b) * 0.5 for a, b in zip(new[::2], new[1::2])]
                for j in range(half):
                    row = LAGS + (level - 1) * half + j
                    fresh.append(
                        edge_ref[slot + offset, row * SUB : (row + 1) * SUB, :]
                        + level_mean_ref[row]
                    )
                new = fresh
            base = level * LAGS
            old = [
                last_ref[slot, (base + i) * SUB : (base + i + 1) * SUB, :]
                for i in range(LAGS)
            ]
            totals = []
            for k in range(1, LAGS + 1):
                row = base + k - 1
                total = totals_ref[slot, row * SUB : (row + 1) * SUB, :]
                for i in range(LAGS - k, LAGS):
                    total = total + old[i] * new[i + k - LAGS]
                totals.append(total)
            upper, base = level // split, (level % split) * LAGS

            def put(ref, totals=totals, base=base):
                for i, total in enumerate(totals):
                    ref[slot, (base + i) * SUB : (base + i + 1) * SUB, :] = total

            pl.when(side == upper)(functools.partial(put, kept_ref))
            pl.when(side != upper)(functools.partial(put, sent_ref))
        return carry

    lax.fori_loop(0, groups, one_group, 0)


def finish_kernel(total_frames, side_ref, mine_ref, got_ref, sum_ref, *refs):
    out_ref = refs[-1]
    split = LEVELS // 2
    g = pl.program_id(0)
    side = side_ref[0]
    for c in range(SUB):
        mean = sum_ref[g, c : c + 1, :] / total_frames
        square = jnp.broadcast_to(mean * mean, (SUB, LANE))
        for level in range(LEVELS):
            own = side == level // split
            for i in range(LAGS // SUB):
                lag = lax.broadcasted_iota(jnp.int32, (SUB, LANE), 0) + (i * SUB + 1)
                count = ((total_frames >> level) - lag).astype(jnp.float32)
                row = (level % split) * LAGS + i * SUB
                at = pl.ds(row * SUB + c, SUB, stride=SUB)
                total = jnp.where(own, mine_ref[g, at, :], got_ref[g, at, :])
                out_ref[level, i * SUB : (i + 1) * SUB, c * LANE : (c + 1) * LANE] = (
                    total / (count * square)
                )


ROWS = LEVELS * LAGS
EDGE_ROWS = LAGS + (LEVELS - 1) * (LAGS // 2)
SMEM = pl.BlockSpec(memory_space=pltpu.SMEM)
VMEM = pl.BlockSpec(memory_space=pltpu.VMEM)


def params():
    return pltpu.CompilerParams(vmem_limit_bytes=VMEM_LIMIT)


def in_hbm(value):
    return pltpu.with_memory_space_constraint(value, pltpu.HBM)


def f32(*shape):
    return jax.ShapeDtypeStruct(shape, jnp.float32)


def by_group(rows):
    return pl.BlockSpec((1, rows * SUB, LANE), lambda g: (g, 0, 0))


def swap(block, mask):
    size = lax.axis_size("tm")
    return lax.ppermute(block, "tm", [(i, i ^ mask) for i in range(size)])


def after(value, token):
    return lax.optimization_barrier((value, token))[0]


class Part:
    def __init__(self, order, uppers, kept, sent):
        self.order = order
        self.uppers = uppers
        self.kept, self.sent = kept, sent
        self.sums = sent[:, kept.shape[1] :]
        steps = len(order)
        self.route = list(range(steps)) + list(reversed(range(steps - 1)))
        self.at = 0
        self.got = swap(sent, order[0])

    def finished(self):
        return self.at == len(self.route) - 1

    def advance(self, token):
        steps = len(self.order)
        got = after(self.got, token)
        if self.at < steps:
            rows = self.kept.shape[1]
            self.cur = self.kept + got[:, :rows]
            self.sums = self.sums + got[:, rows:]
        else:
            upper = self.uppers[self.order[self.route[self.at]]]
            low = jnp.where(upper, got, self.cur)
            high = jnp.where(upper, self.cur, got)
            self.cur = jnp.concatenate([low, high], axis=1)
        self.at += 1
        mask = self.order[self.route[self.at]]
        if self.at < steps:
            if self.at == steps - 1:
                self.kept = self.sent = self.cur
            else:
                half = self.cur.shape[1] // 2
                low, high = self.cur[:, :half], self.cur[:, half:]
                self.kept = jnp.where(self.uppers[mask], high, low)
                self.sent = jnp.where(self.uppers[mask], low, high)
            self.sent = jnp.concatenate([self.sent, self.sums], axis=1)
        else:
            self.sent = self.cur
        self.got = swap(self.sent, mask)
        return self.sent


def plan(groups, bits):
    x, y, z = (bits + bits[-1:] * 2)[:3]
    tail = bits[3:]
    cuts = [groups * i // 8 for i in CUTS]
    orders = [[z, y, x] + tail, [y, x, z] + tail, [x, z, y] + tail]
    orders = [o[: len(bits)] for o in orders]
    return [(a, b - a, o) for a, b, o in zip(cuts, cuts[1:], orders)]


CUTS = (0, 3, 6, 8)


def on_device(frames, ref_weight):
    rows, pixels = frames.shape
    groups = pixels // GROUP
    size = lax.axis_size("tm")
    total_frames = rows * size
    bits = [1 << b for b in range(size.bit_length() - 1)]
    parts = plan(groups, bits)
    me = lax.axis_index("tm")
    uppers = {bit: (me & bit) != 0 for bit in bits}
    sides = {o[0]: uppers[o[0]].astype(jnp.int32).reshape(1) for _, _, o in parts}
    ref_weight, uppers, sides = lax.optimization_barrier((ref_weight, uppers, sides))
    stored = in_hbm(frames)
    head = parts[0][1]
    spans = [(0, head), (head, groups - head)]
    back = [(i, i - 1) for i in range(1, size)]
    sums, *edges = pl.pallas_call(
        functools.partial(edge_kernel, spans),
        in_specs=[pl.BlockSpec(memory_space=pl.ANY)] * 2,
        out_specs=[VMEM] * (1 + len(spans)),
        out_shape=[f32(rows + SUB, 1)]
        + [f32(count, EDGE_ROWS * SUB, LANE) for _, count in spans],
        scratch_shapes=[
            pltpu.VMEM((groups, rows, GROUP), jnp.float32),
            pltpu.VMEM((1, pixels), jnp.float32),
            pltpu.VMEM((rows * SUB, LANE), jnp.float32),
            pltpu.VMEM((rows + SUB, LANE), jnp.float32),
            pltpu.SemaphoreType.DMA((groups,)),
            pltpu.SemaphoreType.DMA,
        ],
        compiler_params=params(),
        name="edges",
    )(stored, in_hbm(ref_weight.reshape(1, pixels)))
    next_edges = [lax.ppermute(edges[0], "tm", back)]
    sums = lax.psum(sums[:, 0], "pix")
    mean = sums[:rows] / sums[rows]
    next_mean = lax.ppermute(mean, "tm", back)
    for edge in edges[1:]:
        next_edges.append(lax.ppermute(after(edge, mean), "tm", back))

    def inner(p, token):
        first, count, _ = parts[p]
        return pl.pallas_call(
            inner_kernel,
            grid=(count,),
            in_specs=[
                SMEM,
                pl.BlockSpec((rows, GROUP), lambda g: (0, g + first)),
            ],
            out_specs=[by_group(ROWS), by_group(ROWS), by_group(1)],
            out_shape=[
                f32(count, ROWS * SUB, LANE),
                f32(count, ROWS * SUB, LANE),
                f32(count, SUB, LANE),
            ],
            scratch_shapes=[
                pltpu.VMEM((rows * SUB, LANE), jnp.float32),
                pltpu.VMEM((rows, LANE), jnp.float32),
            ],
            compiler_params=params(),
            name=f"inner_{p}",
        )(after(mean, token), stored)

    def border(p, sums, token):
        first, count, order = parts[p]
        totals, last, pixel_sum = sums
        kept, sent = pl.pallas_call(
            functools.partial(border_kernel, first - spans[p > 0][0]),
            in_specs=[SMEM, SMEM] + [VMEM] * 4,
            out_specs=[VMEM, VMEM],
            out_shape=[
                f32(count, ROWS // 2 * SUB, LANE),
                f32(count, (ROWS // 2 + 1) * SUB, LANE),
            ],
            scratch_shapes=[pltpu.SMEM((EDGE_ROWS,), jnp.float32)],
            compiler_params=params(),
            name=f"border_{p}",
        )(next_mean, sides[order[0]], after(next_edges[p > 0], token), last, totals, pixel_sum)
        return Part(order, uppers, kept, sent)

    sums = []
    token = mean
    local = []
    for p in range(len(parts)):
        local.append(inner(p, token))
        token = local[p][2]
    for p in range(len(parts)):
        sums.append(border(p, local[p], token))
        token = sums[p].sent
    while not all(part.finished() for part in sums):
        for part in sums:
            if not part.finished():
                token = part.advance(token)
    out = None
    for p, (first, count, order) in enumerate(parts):
        held = [] if out is None else [out]
        part = sums[p]
        out = pl.pallas_call(
            functools.partial(finish_kernel, total_frames),
            grid=(count,),
            in_specs=[SMEM, VMEM, VMEM, VMEM]
            + [pl.BlockSpec(memory_space=pl.ANY)] * len(held),
            out_specs=pl.BlockSpec(
                (LEVELS, LAGS, GROUP), lambda g, first=first: (0, 0, g + first)
            ),
            out_shape=f32(LEVELS, LAGS, pixels),
            input_output_aliases={4: 0} if held else {},
            compiler_params=params(),
            name=f"finish_{p}",
        )(sides[order[0]], part.cur, part.got, part.sums, *held)
    return out


def solution(mesh):
    return jax.shard_map(
        on_device,
        mesh=mesh,
        in_specs=(P("tm", "pix"), P("pix")),
        out_specs=P(None, None, "pix"),
        check_vma=False,
    )
```

```python
import functools

import jax
import jax.numpy as jnp
from jax import lax
from jax.experimental import pallas as pl
from jax.experimental.pallas import tpu as pltpu
from jax.sharding import PartitionSpec as P

LEVELS = 4
LAGS = 16
SUB, LANE = 8, 128
GROUP = SUB * LANE
VMEM_LIMIT = 16 * 1024 * 1024


def tile(ref, row):
    return ref[row * SUB : (row + 1) * SUB, :]


def edge_kernel(spans, x_hbm, w_hbm, sums_ref, *refs):
    edge_refs, refs = refs[: len(spans)], refs[len(spans) :]
    x_ref, w_ref, tall_ref, acc_ref, sem, w_sem = refs
    groups, rows, _ = x_ref.shape
    half = LAGS // 2

    def fetch(g):
        at = pl.ds(pl.multiple_of(g * GROUP, GROUP), GROUP)
        return pltpu.make_async_copy(x_hbm.at[:, at], x_ref.at[g], sem.at[g])

    weights = pltpu.make_async_copy(w_hbm, w_ref, w_sem)
    weights.start()
    for g in range(groups):
        fetch(g).start()
    acc_ref[...] = jnp.zeros_like(acc_ref)
    weights.wait()

    def one_group(first, edge_ref, slot, carry):
        g = slot + first
        fetch(g).wait()
        for c in range(SUB):
            at = pl.ds(pl.multiple_of(g * GROUP + c * LANE, LANE), LANE)
            weight = jnp.broadcast_to(w_ref[:, at], (SUB, LANE))
            acc_ref[rows : rows + SUB, :] += weight
            for i in range(rows // SUB):
                part = slice(i * SUB, (i + 1) * SUB)
                value = x_ref[g, part, c * LANE : (c + 1) * LANE]
                acc_ref[part, :] += value * weight
                tall_ref[pl.ds(i * SUB * SUB + c, SUB, stride=SUB), :] = value
        edge_ref[slot, : LAGS * SUB, :] = tall_ref[: LAGS * SUB, :]
        for level in range(1, LEVELS):
            span = 1 << level
            for j in range(half):
                group = [tile(tall_ref, (half + j) * span + s) for s in range(span)]
                while len(group) > 1:
                    group = [(a + b) * 0.5 for a, b in zip(group[::2], group[1::2])]
                row = LAGS + (level - 1) * half + j
                edge_ref[slot, row * SUB : (row + 1) * SUB, :] = group[0]
        return carry

    for (first, count), edge_ref in zip(spans, edge_refs):
        lax.fori_loop(0, count, functools.partial(one_group, first, edge_ref), 0)
    sums_ref[...] = jnp.sum(acc_ref[...], axis=1, keepdims=True)


def lag_step(read, near, far, totals):
    window = [read(i) for i in range(LAGS)]
    out = list(totals)
    for i in range(near):
        for k in range(1, LAGS + 1):
            if i + k < far:
                if i + k == len(window):
                    window.append(read(i + k))
                out[k - 1] = out[k - 1] + window[i] * window[i + k]
    return out


def inner_kernel(mean_ref, x_ref, totals_ref, last_ref, sum_ref, series_ref, wide_ref):
    rows = x_ref.shape[0]

    @pl.when(pl.program_id(0) == 0)
    def _():
        for t in range(rows):
            wide_ref[t : t + 1, :] = jnp.full((1, LANE), mean_ref[t], jnp.float32)

    for c in range(SUB):
        total = None
        for i in range(rows // SUB):
            part = slice(i * SUB, (i + 1) * SUB)
            value = x_ref[part, c * LANE : (c + 1) * LANE] + wide_ref[part, :]
            series_ref[pl.ds(i * SUB * SUB + c, SUB, stride=SUB), :] = value
            total = value if total is None else total + value
        sum_ref[0, c : c + 1, :] = jnp.sum(total, axis=0, keepdims=True)
    zero = jnp.zeros((SUB, LANE), jnp.float32)
    for level in range(LEVELS):
        count = rows >> level
        chunks = count // LAGS

        def reader(chunk):
            start = chunk * (LAGS * SUB)

            def read(i):
                return series_ref[pl.ds(pl.multiple_of(start + i * SUB, SUB), SUB), :]

            return read

        def body(chunk, totals):
            return tuple(lag_step(reader(chunk), LAGS, 2 * LAGS, totals))

        totals = tuple([zero] * LAGS)
        if chunks > 1:
            totals = lax.fori_loop(0, chunks - 1, body, totals)
        read = reader(chunks - 1)
        totals = lag_step(read, LAGS, LAGS, totals)
        old = [read(i) for i in range(LAGS)]
        for i in range(LAGS):
            row = level * LAGS + i
            totals_ref[0, row * SUB : (row + 1) * SUB, :] = totals[i]
            last_ref[0, row * SUB : (row + 1) * SUB, :] = old[i]
        if level < LEVELS - 1:
            for i in range(count // 2):
                pair = tile(series_ref, 2 * i) + tile(series_ref, 2 * i + 1)
                series_ref[i * SUB : (i + 1) * SUB, :] = pair * 0.5


def border_kernel(offset, mean_ref, side_ref, edge_ref, last_ref, totals_ref,
                  sum_ref, kept_ref, sent_ref, level_mean_ref):
    half = LAGS // 2
    split = LEVELS // 2
    side = side_ref[0]
    groups = kept_ref.shape[0]
    for j in range(LAGS):
        level_mean_ref[j] = mean_ref[j]
    for level in range(1, LEVELS):
        span = 1 << level
        for j in range(half):
            group = [mean_ref[(half + j) * span + s] for s in range(span)]
            while len(group) > 1:
                group = [(a + b) * 0.5 for a, b in zip(group[::2], group[1::2])]
            level_mean_ref[LAGS + (level - 1) * half + j] = group[0]

    def one_group(slot, carry):
        sent_ref[slot, ROWS // 2 * SUB :, :] = sum_ref[slot]
        new = [
            edge_ref[slot + offset, j * SUB : (j + 1) * SUB, :] + level_mean_ref[j]
            for j in range(LAGS)
        ]
        for level in range(LEVELS):
            if level > 0:
                fresh = [(a + b) * 0.5 for a, b in zip(new[::2], new[1::2])]
                for j in range(half):
                    row = LAGS + (level - 1) * half + j
                    fresh.append(
                        edge_ref[slot + offset, row * SUB : (row + 1) * SUB, :]
                        + level_mean_ref[row]
                    )
                new = fresh
            base = level * LAGS
            old = [
                last_ref[slot, (base + i) * SUB : (base + i + 1) * SUB, :]
                for i in range(LAGS)
            ]
            totals = []
            for k in range(1, LAGS + 1):
                row = base + k - 1
                total = totals_ref[slot, row * SUB : (row + 1) * SUB, :]
                for i in range(LAGS - k, LAGS):
                    total = total + old[i] * new[i + k - LAGS]
                totals.append(total)
            upper, base = level // split, (level % split) * LAGS

            def put(ref, totals=totals, base=base):
                for i, total in enumerate(totals):
                    ref[slot, (base + i) * SUB : (base + i + 1) * SUB, :] = total

            pl.when(side == upper)(functools.partial(put, kept_ref))
            pl.when(side != upper)(functools.partial(put, sent_ref))
        return carry

    lax.fori_loop(0, groups, one_group, 0)


def finish_kernel(first, total_frames, side_ref, mine_ref, got_ref, sum_ref, *refs):
    out_hbm, out_ref, sem = refs[-3:]
    split = LEVELS // 2
    groups = mine_ref.shape[0]
    side = side_ref[0]

    def put(g):
        at = pl.ds((first + g) * GROUP, GROUP)
        return pltpu.make_async_copy(out_ref.at[g], out_hbm.at[:, :, at], sem.at[g])

    for g in range(groups):
        for c in range(SUB):
            mean = sum_ref[g, c : c + 1, :] / total_frames
            square = jnp.broadcast_to(mean * mean, (SUB, LANE))
            for level in range(LEVELS):
                own = side == level // split
                for i in range(LAGS // SUB):
                    lag = lax.broadcasted_iota(jnp.int32, (SUB, LANE), 0) + (i * SUB + 1)
                    count = ((total_frames >> level) - lag).astype(jnp.float32)
                    row = (level % split) * LAGS + i * SUB
                    at = pl.ds(row * SUB + c, SUB, stride=SUB)
                    total = jnp.where(own, mine_ref[g, at, :], got_ref[g, at, :])
                    out_ref[
                        g, level, i * SUB : (i + 1) * SUB, c * LANE : (c + 1) * LANE
                    ] = total / (count * square)
        put(g).start()
    for g in range(groups):
        put(g).wait()


ROWS = LEVELS * LAGS
EDGE_ROWS = LAGS + (LEVELS - 1) * (LAGS // 2)
SMEM = pl.BlockSpec(memory_space=pltpu.SMEM)
VMEM = pl.BlockSpec(memory_space=pltpu.VMEM)


def params():
    return pltpu.CompilerParams(vmem_limit_bytes=VMEM_LIMIT)


def in_hbm(value):
    return pltpu.with_memory_space_constraint(value, pltpu.HBM)


def f32(*shape):
    return jax.ShapeDtypeStruct(shape, jnp.float32)


def by_group(rows):
    return pl.BlockSpec((1, rows * SUB, LANE), lambda g: (g, 0, 0))


def swap(block, masks):
    size, cores = lax.axis_size("tm"), lax.axis_size("pix")
    route = [
        (i * cores + c, (i ^ masks[c % 2]) * cores + c)
        for i in range(size)
        for c in range(cores)
    ]
    return lax.ppermute(block, ("tm", "pix"), route)


def after(value, token):
    return lax.optimization_barrier((value, token))[0]


class Part:
    def __init__(self, order, uppers, kept, sent):
        self.order = order
        self.uppers = uppers
        self.kept, self.sent = kept, sent
        self.sums = sent[:, kept.shape[1] :]
        steps = len(order)
        self.route = list(range(steps)) + list(reversed(range(steps - 1)))
        self.at = 0
        self.got = swap(sent, order[0])

    def finished(self):
        return self.at == len(self.route) - 1

    def advance(self, token):
        steps = len(self.order)
        got = after(self.got, token)
        if self.at < steps:
            rows = self.kept.shape[1]
            self.cur = self.kept + got[:, :rows]
            self.sums = self.sums + got[:, rows:]
        else:
            upper = self.uppers[self.order[self.route[self.at]]]
            low = jnp.where(upper, got, self.cur)
            high = jnp.where(upper, self.cur, got)
            self.cur = jnp.concatenate([low, high], axis=1)
        self.at += 1
        mask = self.order[self.route[self.at]]
        if self.at < steps:
            if self.at == steps - 1:
                self.kept = self.sent = self.cur
            else:
                half = self.cur.shape[1] // 2
                low, high = self.cur[:, :half], self.cur[:, half:]
                self.kept = jnp.where(self.uppers[mask], high, low)
                self.sent = jnp.where(self.uppers[mask], low, high)
            self.sent = jnp.concatenate([self.sent, self.sums], axis=1)
        else:
            self.sent = self.cur
        self.got = swap(self.sent, mask)
        return self.sent


def plan(groups, bits):
    x, y, z = (bits + bits[-1:] * 2)[:3]
    cuts = [groups * i // 8 for i in CUTS]
    even = [[y, z, x], [x, y, z], [z, x, y]]
    odd = [[x, y, z], [z, x, y], [y, z, x]]
    orders = [list(zip(e + bits[3:], o + bits[3:])) for e, o in zip(even, odd)]
    orders = [o[: len(bits)] for o in orders]
    return [(a, b - a, o) for a, b, o in zip(cuts, cuts[1:], orders)]


CUTS = (0, 3, 6, 8)


def on_device(frames, ref_weight):
    rows, pixels = frames.shape
    groups = pixels // GROUP
    size = lax.axis_size("tm")
    total_frames = rows * size
    bits = [1 << b for b in range(size.bit_length() - 1)]
    parts = plan(groups, bits)
    me = lax.axis_index("tm")
    odd = lax.axis_index("pix") % 2 == 1
    uppers = {
        masks: (me & jnp.where(odd, masks[1], masks[0])) != 0
        for _, _, order in parts
        for masks in order
    }
    sides = {o[0]: uppers[o[0]].astype(jnp.int32).reshape(1) for _, _, o in parts}
    ref_weight, uppers, sides = lax.optimization_barrier((ref_weight, uppers, sides))
    stored = in_hbm(frames)
    head = parts[0][1]
    spans = [(0, head), (head, groups - head)]
    back = [(i, i - 1) for i in range(1, size)]
    sums, *edges = pl.pallas_call(
        functools.partial(edge_kernel, spans),
        in_specs=[pl.BlockSpec(memory_space=pl.ANY)] * 2,
        out_specs=[VMEM] * (1 + len(spans)),
        out_shape=[f32(rows + SUB, 1)]
        + [f32(count, EDGE_ROWS * SUB, LANE) for _, count in spans],
        scratch_shapes=[
            pltpu.VMEM((groups, rows, GROUP), jnp.float32),
            pltpu.VMEM((1, pixels), jnp.float32),
            pltpu.VMEM((rows * SUB, LANE), jnp.float32),
            pltpu.VMEM((rows + SUB, LANE), jnp.float32),
            pltpu.SemaphoreType.DMA((groups,)),
            pltpu.SemaphoreType.DMA,
        ],
        compiler_params=params(),
        name="edges",
    )(stored, in_hbm(ref_weight.reshape(1, pixels)))
    next_edges = [lax.ppermute(edges[0], "tm", back)]
    sums = lax.psum(sums[:, 0], "pix")
    mean = sums[:rows] / sums[rows]
    next_mean = lax.ppermute(mean, "tm", back)
    for edge in edges[1:]:
        next_edges.append(lax.ppermute(after(edge, mean), "tm", back))

    def inner(p, token):
        first, count, _ = parts[p]
        return pl.pallas_call(
            inner_kernel,
            grid=(count,),
            in_specs=[
                SMEM,
                pl.BlockSpec((rows, GROUP), lambda g: (0, g + first)),
            ],
            out_specs=[by_group(ROWS), by_group(ROWS), by_group(1)],
            out_shape=[
                f32(count, ROWS * SUB, LANE),
                f32(count, ROWS * SUB, LANE),
                f32(count, SUB, LANE),
            ],
            scratch_shapes=[
                pltpu.VMEM((rows * SUB, LANE), jnp.float32),
                pltpu.VMEM((rows, LANE), jnp.float32),
            ],
            compiler_params=params(),
            name=f"inner_{p}",
        )(after(mean, token), stored)

    def border(p, sums, token):
        first, count, order = parts[p]
        totals, last, pixel_sum = sums
        kept, sent = pl.pallas_call(
            functools.partial(border_kernel, first - spans[p > 0][0]),
            in_specs=[SMEM, SMEM] + [VMEM] * 4,
            out_specs=[VMEM, VMEM],
            out_shape=[
                f32(count, ROWS // 2 * SUB, LANE),
                f32(count, (ROWS // 2 + 1) * SUB, LANE),
            ],
            scratch_shapes=[pltpu.SMEM((EDGE_ROWS,), jnp.float32)],
            compiler_params=params(),
            name=f"border_{p}",
        )(next_mean, sides[order[0]], after(next_edges[p > 0], token), last, totals, pixel_sum)
        return Part(order, uppers, kept, sent)

    sums = []
    token = mean
    local = []
    for p in range(len(parts)):
        local.append(inner(p, token))
        token = local[p][2]
    for p in range(len(parts)):
        sums.append(border(p, local[p], token))
        token = sums[p].sent
    while not all(part.finished() for part in sums):
        for part in sums:
            if not part.finished():
                token = part.advance(token)
    out = None
    for p, (first, count, order) in enumerate(parts):
        held = [] if out is None else [out]
        part = sums[p]
        out = pl.pallas_call(
            functools.partial(finish_kernel, first, total_frames),
            in_specs=[SMEM, VMEM, VMEM, VMEM]
            + [pl.BlockSpec(memory_space=pl.ANY)] * len(held),
            out_specs=pl.BlockSpec(memory_space=pl.ANY),
            out_shape=f32(LEVELS, LAGS, pixels),
            scratch_shapes=[
                pltpu.VMEM((count, LEVELS, LAGS, GROUP), jnp.float32),
                pltpu.SemaphoreType.DMA((count,)),
            ],
            input_output_aliases={4: 0} if held else {},
            compiler_params=params(),
            name=f"finish_{p}",
        )(sides[order[0]], part.cur, part.got, part.sums, *held)
    return out


def solution(mesh):
    return jax.shard_map(
        on_device,
        mesh=mesh,
        in_specs=(P("tm", "pix"), P("pix")),
        out_specs=P(None, None, "pix"),
        check_vma=False,
    )
```

```python
import functools

import jax
import jax.numpy as jnp
from jax import lax
from jax.experimental import pallas as pl
from jax.experimental.pallas import tpu as pltpu
from jax.sharding import PartitionSpec as P

LEVELS = 4
LAGS = 16
SUB, LANE = 8, 128
GROUP = SUB * LANE
VMEM_LIMIT = 16 * 1024 * 1024


def tile(ref, row):
    return ref[row * SUB : (row + 1) * SUB, :]


def edge_kernel(first, x_hbm, w_hbm, sums_ref, edge_ref, x_ref, w_ref, tall_ref, acc_ref, sem, w_sem):
    groups, rows, _ = x_ref.shape
    half = LAGS // 2

    def fetch(g):
        at = pl.ds(pl.multiple_of((first + g) * GROUP, GROUP), GROUP)
        return pltpu.make_async_copy(x_hbm.at[:, at], x_ref.at[g], sem.at[g])

    weights = pltpu.make_async_copy(w_hbm, w_ref, w_sem)
    weights.start()
    for g in range(groups):
        fetch(g).start()
    acc_ref[...] = jnp.zeros_like(acc_ref)
    weights.wait()

    def one_group(g, carry):
        fetch(g).wait()
        for c in range(SUB):
            at = pl.ds(pl.multiple_of((first + g) * GROUP + c * LANE, LANE), LANE)
            weight = jnp.broadcast_to(w_ref[:, at], (SUB, LANE))
            acc_ref[rows : rows + SUB, :] += weight
            for i in range(rows // SUB):
                part = slice(i * SUB, (i + 1) * SUB)
                value = x_ref[g, part, c * LANE : (c + 1) * LANE]
                acc_ref[part, :] += value * weight
                tall_ref[pl.ds(i * SUB * SUB + c, SUB, stride=SUB), :] = value
        edge_ref[g, : LAGS * SUB, :] = tall_ref[: LAGS * SUB, :]
        for level in range(1, LEVELS):
            span = 1 << level
            for j in range(half):
                group = [tile(tall_ref, (half + j) * span + s) for s in range(span)]
                while len(group) > 1:
                    group = [(a + b) * 0.5 for a, b in zip(group[::2], group[1::2])]
                row = LAGS + (level - 1) * half + j
                edge_ref[g, row * SUB : (row + 1) * SUB, :] = group[0]
        return carry

    lax.fori_loop(0, groups, one_group, 0)
    sums_ref[...] = jnp.sum(acc_ref[...], axis=1, keepdims=True)


def lag_step(read, near, far, totals):
    window = [read(i) for i in range(LAGS)]
    out = list(totals)
    for i in range(near):
        for k in range(1, LAGS + 1):
            if i + k < far:
                if i + k == len(window):
                    window.append(read(i + k))
                out[k - 1] = out[k - 1] + window[i] * window[i + k]
    return out


def inner_kernel(mean_ref, x_ref, totals_ref, last_ref, sum_ref, series_ref, wide_ref):
    rows = x_ref.shape[0]

    @pl.when(pl.program_id(0) == 0)
    def _():
        for t in range(rows):
            wide_ref[t : t + 1, :] = jnp.full((1, LANE), mean_ref[t], jnp.float32)

    for c in range(SUB):
        total = None
        for i in range(rows // SUB):
            part = slice(i * SUB, (i + 1) * SUB)
            value = x_ref[part, c * LANE : (c + 1) * LANE] + wide_ref[part, :]
            series_ref[pl.ds(i * SUB * SUB + c, SUB, stride=SUB), :] = value
            total = value if total is None else total + value
        sum_ref[0, c : c + 1, :] = jnp.sum(total, axis=0, keepdims=True)
    zero = jnp.zeros((SUB, LANE), jnp.float32)
    for level in range(LEVELS):
        count = rows >> level
        chunks = count // LAGS

        def reader(chunk):
            start = chunk * (LAGS * SUB)

            def read(i):
                return series_ref[pl.ds(pl.multiple_of(start + i * SUB, SUB), SUB), :]

            return read

        def body(chunk, totals):
            return tuple(lag_step(reader(chunk), LAGS, 2 * LAGS, totals))

        totals = tuple([zero] * LAGS)
        if chunks > 1:
            totals = lax.fori_loop(0, chunks - 1, body, totals)
        read = reader(chunks - 1)
        totals = lag_step(read, LAGS, LAGS, totals)
        old = [read(i) for i in range(LAGS)]
        for i in range(LAGS):
            row = level * LAGS + i
            totals_ref[0, row * SUB : (row + 1) * SUB, :] = totals[i]
            last_ref[0, row * SUB : (row + 1) * SUB, :] = old[i]
        if level < LEVELS - 1:
            for i in range(count // 2):
                pair = tile(series_ref, 2 * i) + tile(series_ref, 2 * i + 1)
                series_ref[i * SUB : (i + 1) * SUB, :] = pair * 0.5


def border_kernel(offset, mean_ref, side_ref, edge_ref, last_ref, totals_ref,
                  sum_ref, kept_ref, sent_ref, level_mean_ref):
    half = LAGS // 2
    split = LEVELS // 2
    side = side_ref[0]
    groups = kept_ref.shape[0]
    for j in range(LAGS):
        level_mean_ref[j] = mean_ref[j]
    for level in range(1, LEVELS):
        span = 1 << level
        for j in range(half):
            group = [mean_ref[(half + j) * span + s] for s in range(span)]
            while len(group) > 1:
                group = [(a + b) * 0.5 for a, b in zip(group[::2], group[1::2])]
            level_mean_ref[LAGS + (level - 1) * half + j] = group[0]

    def one_group(slot, carry):
        sent_ref[slot, ROWS // 2 * SUB :, :] = sum_ref[slot]
        new = [
            edge_ref[slot + offset, j * SUB : (j + 1) * SUB, :] + level_mean_ref[j]
            for j in range(LAGS)
        ]
        for level in range(LEVELS):
            if level > 0:
                fresh = [(a + b) * 0.5 for a, b in zip(new[::2], new[1::2])]
                for j in range(half):
                    row = LAGS + (level - 1) * half + j
                    fresh.append(
                        edge_ref[slot + offset, row * SUB : (row + 1) * SUB, :]
                        + level_mean_ref[row]
                    )
                new = fresh
            base = level * LAGS
            old = [
                last_ref[slot, (base + i) * SUB : (base + i + 1) * SUB, :]
                for i in range(LAGS)
            ]
            totals = []
            for k in range(1, LAGS + 1):
                row = base + k - 1
                total = totals_ref[slot, row * SUB : (row + 1) * SUB, :]
                for i in range(LAGS - k, LAGS):
                    total = total + old[i] * new[i + k - LAGS]
                totals.append(total)
            upper, base = level // split, (level % split) * LAGS

            def put(ref, totals=totals, base=base):
                for i, total in enumerate(totals):
                    ref[slot, (base + i) * SUB : (base + i + 1) * SUB, :] = total

            pl.when(side == upper)(functools.partial(put, kept_ref))
            pl.when(side != upper)(functools.partial(put, sent_ref))
        return carry

    lax.fori_loop(0, groups, one_group, 0)


def finish_kernel(first, total_frames, side_ref, mine_ref, got_ref, sum_ref, *refs):
    out_hbm, out_ref, sem = refs[-3:]
    split = LEVELS // 2
    groups = mine_ref.shape[0]
    side = side_ref[0]

    def put(g):
        at = pl.ds((first + g) * GROUP, GROUP)
        return pltpu.make_async_copy(out_ref.at[g], out_hbm.at[:, :, at], sem.at[g])

    for g in range(groups):
        for c in range(SUB):
            mean = sum_ref[g, c : c + 1, :] / total_frames
            square = jnp.broadcast_to(mean * mean, (SUB, LANE))
            for level in range(LEVELS):
                own = side == level // split
                for i in range(LAGS // SUB):
                    lag = lax.broadcasted_iota(jnp.int32, (SUB, LANE), 0) + (i * SUB + 1)
                    count = ((total_frames >> level) - lag).astype(jnp.float32)
                    row = (level % split) * LAGS + i * SUB
                    at = pl.ds(row * SUB + c, SUB, stride=SUB)
                    total = jnp.where(own, mine_ref[g, at, :], got_ref[g, at, :])
                    out_ref[
                        g, level, i * SUB : (i + 1) * SUB, c * LANE : (c + 1) * LANE
                    ] = total / (count * square)
        put(g).start()
    for g in range(groups):
        put(g).wait()


ROWS = LEVELS * LAGS
EDGE_ROWS = LAGS + (LEVELS - 1) * (LAGS // 2)
SMEM = pl.BlockSpec(memory_space=pltpu.SMEM)
VMEM = pl.BlockSpec(memory_space=pltpu.VMEM)


def params():
    return pltpu.CompilerParams(vmem_limit_bytes=VMEM_LIMIT)


def in_hbm(value):
    return pltpu.with_memory_space_constraint(value, pltpu.HBM)


def f32(*shape):
    return jax.ShapeDtypeStruct(shape, jnp.float32)


def by_group(rows):
    return pl.BlockSpec((1, rows * SUB, LANE), lambda g: (g, 0, 0))


def swap(block, masks):
    size, cores = lax.axis_size("tm"), lax.axis_size("pix")
    route = [
        (i * cores + c, (i ^ masks[c % 2]) * cores + c)
        for i in range(size)
        for c in range(cores)
    ]
    return lax.ppermute(block, ("tm", "pix"), route)


def after(value, token):
    return lax.optimization_barrier((value, token))[0]


class Part:
    def __init__(self, order, uppers, kept, sent):
        self.order = order
        self.uppers = uppers
        self.kept, self.sent = kept, sent
        self.sums = sent[:, kept.shape[1] :]
        steps = len(order)
        self.route = list(range(steps)) + list(reversed(range(steps - 1)))
        self.at = 0
        self.got = swap(sent, order[0])

    def finished(self):
        return self.at == len(self.route) - 1

    def advance(self, token):
        steps = len(self.order)
        got = after(self.got, token)
        if self.at < steps:
            rows = self.kept.shape[1]
            self.cur = self.kept + got[:, :rows]
            self.sums = self.sums + got[:, rows:]
        else:
            upper = self.uppers[self.order[self.route[self.at]]]
            low = jnp.where(upper, got, self.cur)
            high = jnp.where(upper, self.cur, got)
            self.cur = jnp.concatenate([low, high], axis=1)
        self.at += 1
        mask = self.order[self.route[self.at]]
        if self.at < steps:
            if self.at == steps - 1:
                self.kept = self.sent = self.cur
            else:
                half = self.cur.shape[1] // 2
                low, high = self.cur[:, :half], self.cur[:, half:]
                self.kept = jnp.where(self.uppers[mask], high, low)
                self.sent = jnp.where(self.uppers[mask], low, high)
            self.sent = jnp.concatenate([self.sent, self.sums], axis=1)
        else:
            self.sent = self.cur
        self.got = swap(self.sent, mask)
        return self.sent


def plan(groups, bits):
    x, y, z = (bits + bits[-1:] * 2)[:3]
    cuts = [groups * i // 8 for i in CUTS]
    even = [[y, z, x], [x, y, z], [z, x, y]]
    odd = [[x, y, z], [z, x, y], [y, z, x]]
    orders = [list(zip(e + bits[3:], o + bits[3:])) for e, o in zip(even, odd)]
    orders = [o[: len(bits)] for o in orders]
    return [(a, b - a, o) for a, b, o in zip(cuts, cuts[1:], orders)]


CUTS = (0, 3, 6, 8)


def on_device(frames, ref_weight):
    rows, pixels = frames.shape
    groups = pixels // GROUP
    size = lax.axis_size("tm")
    total_frames = rows * size
    bits = [1 << b for b in range(size.bit_length() - 1)]
    parts = plan(groups, bits)
    me = lax.axis_index("tm")
    odd = lax.axis_index("pix") % 2 == 1
    uppers = {
        masks: (me & jnp.where(odd, masks[1], masks[0])) != 0
        for _, _, order in parts
        for masks in order
    }
    sides = {o[0]: uppers[o[0]].astype(jnp.int32).reshape(1) for _, _, o in parts}
    ref_weight, uppers, sides = lax.optimization_barrier((ref_weight, uppers, sides))
    stored = in_hbm(frames)
    head = parts[0][1]
    spans = [(0, head), (head, groups - head)]
    back = [(i, i - 1) for i in range(1, size)]
    all_sums, edges = [], []
    for p, (first, count) in enumerate(spans):
        source = stored if p == 0 else in_hbm(after(frames, all_sums[0]))
        sums, edge = pl.pallas_call(
            functools.partial(edge_kernel, first),
            in_specs=[pl.BlockSpec(memory_space=pl.ANY)] * 2,
            out_specs=[VMEM, VMEM],
            out_shape=[f32(rows + SUB, 1), f32(count, EDGE_ROWS * SUB, LANE)],
            scratch_shapes=[
                pltpu.VMEM((count, rows, GROUP), jnp.float32),
                pltpu.VMEM((1, pixels), jnp.float32),
                pltpu.VMEM((rows * SUB, LANE), jnp.float32),
                pltpu.VMEM((rows + SUB, LANE), jnp.float32),
                pltpu.SemaphoreType.DMA((count,)),
                pltpu.SemaphoreType.DMA,
            ],
            compiler_params=params(),
            name=f"edges_{p}",
        )(source, in_hbm(ref_weight.reshape(1, pixels)))
        all_sums.append(sums)
        edges.append(edge)
    sums = sum(all_sums[1:], all_sums[0])
    next_edges = [lax.ppermute(edges[0], "tm", back)]
    sums = lax.psum(sums[:, 0], "pix")
    mean = sums[:rows] / sums[rows]
    next_mean = lax.ppermute(mean, "tm", back)
    for edge in edges[1:]:
        next_edges.append(lax.ppermute(after(edge, mean), "tm", back))

    def inner(p, token):
        first, count, _ = parts[p]
        return pl.pallas_call(
            inner_kernel,
            grid=(count,),
            in_specs=[
                SMEM,
                pl.BlockSpec((rows, GROUP), lambda g: (0, g + first)),
            ],
            out_specs=[by_group(ROWS), by_group(ROWS), by_group(1)],
            out_shape=[
                f32(count, ROWS * SUB, LANE),
                f32(count, ROWS * SUB, LANE),
                f32(count, SUB, LANE),
            ],
            scratch_shapes=[
                pltpu.VMEM((rows * SUB, LANE), jnp.float32),
                pltpu.VMEM((rows, LANE), jnp.float32),
            ],
            compiler_params=params(),
            name=f"inner_{p}",
        )(after(mean, token), stored)

    def border(p, sums, token):
        first, count, order = parts[p]
        totals, last, pixel_sum = sums
        kept, sent = pl.pallas_call(
            functools.partial(border_kernel, first - spans[p > 0][0]),
            in_specs=[SMEM, SMEM] + [VMEM] * 4,
            out_specs=[VMEM, VMEM],
            out_shape=[
                f32(count, ROWS // 2 * SUB, LANE),
                f32(count, (ROWS // 2 + 1) * SUB, LANE),
            ],
            scratch_shapes=[pltpu.SMEM((EDGE_ROWS,), jnp.float32)],
            compiler_params=params(),
            name=f"border_{p}",
        )(next_mean, sides[order[0]], after(next_edges[p > 0], token), last, totals, pixel_sum)
        return Part(order, uppers, kept, sent)

    sums = []
    token = mean
    local = []
    for p in range(len(parts)):
        local.append(inner(p, token))
        token = local[p][2]
    for p in range(len(parts)):
        sums.append(border(p, local[p], token))
        token = sums[p].sent
    while not all(part.finished() for part in sums):
        for part in sums:
            if not part.finished():
                token = part.advance(token)
    out = None
    for p, (first, count, order) in enumerate(parts):
        held = [] if out is None else [out]
        part = sums[p]
        out = pl.pallas_call(
            functools.partial(finish_kernel, first, total_frames),
            in_specs=[SMEM, VMEM, VMEM, VMEM]
            + [pl.BlockSpec(memory_space=pl.ANY)] * len(held),
            out_specs=pl.BlockSpec(memory_space=pl.ANY),
            out_shape=f32(LEVELS, LAGS, pixels),
            scratch_shapes=[
                pltpu.VMEM((count, LEVELS, LAGS, GROUP), jnp.float32),
                pltpu.SemaphoreType.DMA((count,)),
            ],
            input_output_aliases={4: 0} if held else {},
            compiler_params=params(),
            name=f"finish_{p}",
        )(sides[order[0]], part.cur, part.got, part.sums, *held)
    return out


def solution(mesh):
    return jax.shard_map(
        on_device,
        mesh=mesh,
        in_specs=(P("tm", "pix"), P("pix")),
        out_specs=P(None, None, "pix"),
        check_vma=False,
    )
```

```python
import functools

import jax
import jax.numpy as jnp
from jax import lax
from jax.experimental import pallas as pl
from jax.experimental.pallas import tpu as pltpu
from jax.sharding import PartitionSpec as P

LEVELS = 4
LAGS = 16
SUB, LANE = 8, 128
GROUP = SUB * LANE
VMEM_LIMIT = 16 * 1024 * 1024


def tile(ref, row):
    return ref[row * SUB : (row + 1) * SUB, :]


def edge_kernel(first, x_hbm, w_hbm, sums_ref, edge_ref, x_ref, w_ref, tall_ref, acc_ref, sem, w_sem):
    groups, rows, _ = x_ref.shape
    half = LAGS // 2

    def fetch(g):
        at = pl.ds(pl.multiple_of((first + g) * GROUP, GROUP), GROUP)
        return pltpu.make_async_copy(x_hbm.at[:, at], x_ref.at[g], sem.at[g])

    weights = pltpu.make_async_copy(w_hbm, w_ref, w_sem)
    weights.start()
    for g in range(groups):
        fetch(g).start()
    acc_ref[...] = jnp.zeros_like(acc_ref)
    weights.wait()

    def one_group(g, carry):
        fetch(g).wait()
        for c in range(SUB):
            at = pl.ds(pl.multiple_of((first + g) * GROUP + c * LANE, LANE), LANE)
            weight = jnp.broadcast_to(w_ref[:, at], (SUB, LANE))
            acc_ref[rows : rows + SUB, :] += weight
            for i in range(rows // SUB):
                part = slice(i * SUB, (i + 1) * SUB)
                value = x_ref[g, part, c * LANE : (c + 1) * LANE]
                acc_ref[part, :] += value * weight
                tall_ref[pl.ds(i * SUB * SUB + c, SUB, stride=SUB), :] = value
        edge_ref[g, : LAGS * SUB, :] = tall_ref[: LAGS * SUB, :]
        for level in range(1, LEVELS):
            span = 1 << level
            for j in range(half):
                group = [tile(tall_ref, (half + j) * span + s) for s in range(span)]
                while len(group) > 1:
                    group = [(a + b) * 0.5 for a, b in zip(group[::2], group[1::2])]
                row = LAGS + (level - 1) * half + j
                edge_ref[g, row * SUB : (row + 1) * SUB, :] = group[0]
        return carry

    lax.fori_loop(0, groups, one_group, 0)
    sums_ref[...] = jnp.sum(acc_ref[...], axis=1, keepdims=True)


def lag_step(read, near, far, totals):
    window = [read(i) for i in range(LAGS)]
    out = list(totals)
    for i in range(near):
        for k in range(1, LAGS + 1):
            if i + k < far:
                if i + k == len(window):
                    window.append(read(i + k))
                out[k - 1] = out[k - 1] + window[i] * window[i + k]
    return out


def inner_kernel(mean_ref, x_ref, totals_ref, last_ref, sum_ref, series_ref, wide_ref):
    rows = x_ref.shape[0]

    @pl.when(pl.program_id(0) == 0)
    def _():
        for t in range(rows):
            wide_ref[t : t + 1, :] = jnp.full((1, LANE), mean_ref[t], jnp.float32)

    for c in range(SUB):
        total = None
        for i in range(rows // SUB):
            part = slice(i * SUB, (i + 1) * SUB)
            value = x_ref[part, c * LANE : (c + 1) * LANE] + wide_ref[part, :]
            series_ref[pl.ds(i * SUB * SUB + c, SUB, stride=SUB), :] = value
            total = value if total is None else total + value
        sum_ref[0, c : c + 1, :] = jnp.sum(total, axis=0, keepdims=True)
    zero = jnp.zeros((SUB, LANE), jnp.float32)
    for level in range(LEVELS):
        count = rows >> level
        chunks = count // LAGS

        def reader(chunk):
            start = chunk * (LAGS * SUB)

            def read(i):
                return series_ref[pl.ds(pl.multiple_of(start + i * SUB, SUB), SUB), :]

            return read

        def body(chunk, totals):
            return tuple(lag_step(reader(chunk), LAGS, 2 * LAGS, totals))

        totals = tuple([zero] * LAGS)
        if chunks > 1:
            totals = lax.fori_loop(0, chunks - 1, body, totals)
        read = reader(chunks - 1)
        totals = lag_step(read, LAGS, LAGS, totals)
        old = [read(i) for i in range(LAGS)]
        for i in range(LAGS):
            row = level * LAGS + i
            totals_ref[0, row * SUB : (row + 1) * SUB, :] = totals[i]
            last_ref[0, row * SUB : (row + 1) * SUB, :] = old[i]
        if level < LEVELS - 1:
            for i in range(count // 2):
                pair = tile(series_ref, 2 * i) + tile(series_ref, 2 * i + 1)
                series_ref[i * SUB : (i + 1) * SUB, :] = pair * 0.5


def border_kernel(offset, mean_ref, side_ref, edge_ref, last_ref, totals_ref,
                  sum_ref, kept_ref, sent_ref, level_mean_ref):
    half = LAGS // 2
    split = LEVELS // 2
    side = side_ref[0]
    groups = kept_ref.shape[0]
    for j in range(LAGS):
        level_mean_ref[j] = mean_ref[j]
    for level in range(1, LEVELS):
        span = 1 << level
        for j in range(half):
            group = [mean_ref[(half + j) * span + s] for s in range(span)]
            while len(group) > 1:
                group = [(a + b) * 0.5 for a, b in zip(group[::2], group[1::2])]
            level_mean_ref[LAGS + (level - 1) * half + j] = group[0]

    def one_group(slot, carry):
        sent_ref[slot, ROWS // 2 * SUB :, :] = sum_ref[slot]
        new = [
            edge_ref[slot + offset, j * SUB : (j + 1) * SUB, :] + level_mean_ref[j]
            for j in range(LAGS)
        ]
        for level in range(LEVELS):
            if level > 0:
                fresh = [(a + b) * 0.5 for a, b in zip(new[::2], new[1::2])]
                for j in range(half):
                    row = LAGS + (level - 1) * half + j
                    fresh.append(
                        edge_ref[slot + offset, row * SUB : (row + 1) * SUB, :]
                        + level_mean_ref[row]
                    )
                new = fresh
            base = level * LAGS
            old = [
                last_ref[slot, (base + i) * SUB : (base + i + 1) * SUB, :]
                for i in range(LAGS)
            ]
            totals = []
            for k in range(1, LAGS + 1):
                row = base + k - 1
                total = totals_ref[slot, row * SUB : (row + 1) * SUB, :]
                for i in range(LAGS - k, LAGS):
                    total = total + old[i] * new[i + k - LAGS]
                totals.append(total)
            upper, base = level // split, (level % split) * LAGS

            def put(ref, totals=totals, base=base):
                for i, total in enumerate(totals):
                    ref[slot, (base + i) * SUB : (base + i + 1) * SUB, :] = total

            pl.when(side == upper)(functools.partial(put, kept_ref))
            pl.when(side != upper)(functools.partial(put, sent_ref))
        return carry

    lax.fori_loop(0, groups, one_group, 0)


def finish_kernel(first, total_frames, side_ref, mine_ref, got_ref, sum_ref, *refs):
    out_hbm, out_ref, sem = refs[-3:]
    split = LEVELS // 2
    groups = mine_ref.shape[0]
    side = side_ref[0]

    def put(g):
        at = pl.ds((first + g) * GROUP, GROUP)
        return pltpu.make_async_copy(out_ref.at[g], out_hbm.at[:, :, at], sem.at[g])

    for g in range(groups):
        for c in range(SUB):
            mean = sum_ref[g, c : c + 1, :] / total_frames
            square = jnp.broadcast_to(mean * mean, (SUB, LANE))
            for level in range(LEVELS):
                own = side == level // split
                for i in range(LAGS // SUB):
                    lag = lax.broadcasted_iota(jnp.int32, (SUB, LANE), 0) + (i * SUB + 1)
                    count = ((total_frames >> level) - lag).astype(jnp.float32)
                    row = (level % split) * LAGS + i * SUB
                    at = pl.ds(row * SUB + c, SUB, stride=SUB)
                    total = jnp.where(own, mine_ref[g, at, :], got_ref[g, at, :])
                    out_ref[
                        g, level, i * SUB : (i + 1) * SUB, c * LANE : (c + 1) * LANE
                    ] = total / (count * square)
        put(g).start()
    for g in range(groups):
        put(g).wait()


ROWS = LEVELS * LAGS
EDGE_ROWS = LAGS + (LEVELS - 1) * (LAGS // 2)
SMEM = pl.BlockSpec(memory_space=pltpu.SMEM)
VMEM = pl.BlockSpec(memory_space=pltpu.VMEM)


def params():
    return pltpu.CompilerParams(vmem_limit_bytes=VMEM_LIMIT)


def in_hbm(value):
    return pltpu.with_memory_space_constraint(value, pltpu.HBM)


def f32(*shape):
    return jax.ShapeDtypeStruct(shape, jnp.float32)


def by_group(rows):
    return pl.BlockSpec((1, rows * SUB, LANE), lambda g: (g, 0, 0))


def swap(block, masks):
    size, cores = lax.axis_size("tm"), lax.axis_size("pix")
    route = [
        (i * cores + c, (i ^ masks[c % 2]) * cores + c)
        for i in range(size)
        for c in range(cores)
    ]
    return lax.ppermute(block, ("tm", "pix"), route)


def after(value, token):
    return lax.optimization_barrier((value, token))[0]


class Part:
    def __init__(self, order, uppers, kept, sent):
        self.order = order
        self.uppers = uppers
        self.kept, self.sent = kept, sent
        self.sums = sent[:, kept.shape[1] :]
        steps = len(order)
        self.route = list(range(steps)) + list(reversed(range(steps - 1)))
        self.at = 0
        self.got = swap(sent, order[0])

    def finished(self):
        return self.at == len(self.route) - 1

    def advance(self, token):
        steps = len(self.order)
        got = after(self.got, token)
        if self.at < steps:
            rows = self.kept.shape[1]
            self.cur = self.kept + got[:, :rows]
            self.sums = self.sums + got[:, rows:]
        else:
            upper = self.uppers[self.order[self.route[self.at]]]
            low = jnp.where(upper, got, self.cur)
            high = jnp.where(upper, self.cur, got)
            self.cur = jnp.concatenate([low, high], axis=1)
        self.at += 1
        mask = self.order[self.route[self.at]]
        if self.at < steps:
            if self.at == steps - 1:
                self.kept = self.sent = self.cur
            else:
                half = self.cur.shape[1] // 2
                low, high = self.cur[:, :half], self.cur[:, half:]
                self.kept = jnp.where(self.uppers[mask], high, low)
                self.sent = jnp.where(self.uppers[mask], low, high)
            self.sent = jnp.concatenate([self.sent, self.sums], axis=1)
        else:
            self.sent = self.cur
        self.got = swap(self.sent, mask)
        return self.sent


def plan(groups, bits):
    x, y, z = (bits + bits[-1:] * 2)[:3]
    cuts = [groups * i // 8 for i in CUTS]
    even = [[y, z, x], [x, y, z], [z, x, y]]
    odd = [[x, y, z], [z, x, y], [y, z, x]]
    orders = [list(zip(e + bits[3:], o + bits[3:])) for e, o in zip(even, odd)]
    orders = [o[: len(bits)] for o in orders]
    return [(a, b - a, o) for a, b, o in zip(cuts, cuts[1:], orders)]


CUTS = (0, 3, 6, 8)


def on_device(frames, ref_weight):
    rows, pixels = frames.shape
    groups = pixels // GROUP
    size = lax.axis_size("tm")
    total_frames = rows * size
    bits = [1 << b for b in range(size.bit_length() - 1)]
    parts = plan(groups, bits)
    me = lax.axis_index("tm")
    odd = lax.axis_index("pix") % 2 == 1
    uppers = {
        masks: (me & jnp.where(odd, masks[1], masks[0])) != 0
        for _, _, order in parts
        for masks in order
    }
    sides = {o[0]: uppers[o[0]].astype(jnp.int32).reshape(1) for _, _, o in parts}
    ref_weight, uppers, sides = lax.optimization_barrier((ref_weight, uppers, sides))
    stored = in_hbm(frames)
    cut = parts[-1][0]
    spans = [(cut, groups - cut), (0, cut)]
    span_of = [1] * (len(parts) - 1) + [0]
    back = [(i, i - 1) for i in range(1, size)]
    all_sums, edges = [], []
    for p, (first, count) in enumerate(spans):
        source = stored if p == 0 else in_hbm(after(frames, all_sums[0]))
        sums, edge = pl.pallas_call(
            functools.partial(edge_kernel, first),
            in_specs=[pl.BlockSpec(memory_space=pl.ANY)] * 2,
            out_specs=[VMEM, VMEM],
            out_shape=[f32(rows + SUB, 1), f32(count, EDGE_ROWS * SUB, LANE)],
            scratch_shapes=[
                pltpu.VMEM((count, rows, GROUP), jnp.float32),
                pltpu.VMEM((1, pixels), jnp.float32),
                pltpu.VMEM((rows * SUB, LANE), jnp.float32),
                pltpu.VMEM((rows + SUB, LANE), jnp.float32),
                pltpu.SemaphoreType.DMA((count,)),
                pltpu.SemaphoreType.DMA,
            ],
            compiler_params=params(),
            name=f"edges_{p}",
        )(source, in_hbm(ref_weight.reshape(1, pixels)))
        all_sums.append(sums)
        edges.append(edge)
    sums = sum(all_sums[1:], all_sums[0])
    next_edges = [lax.ppermute(edges[0], "tm", back)]
    sums = lax.psum(sums[:, 0], "pix")
    mean = sums[:rows] / sums[rows]
    next_mean = lax.ppermute(mean, "tm", back)
    for edge in edges[1:]:
        next_edges.append(lax.ppermute(after(edge, mean), "tm", back))

    def inner(p, token):
        first, count, _ = parts[p]
        return pl.pallas_call(
            inner_kernel,
            grid=(count,),
            in_specs=[
                SMEM,
                pl.BlockSpec((rows, GROUP), lambda g: (0, g + first)),
            ],
            out_specs=[by_group(ROWS), by_group(ROWS), by_group(1)],
            out_shape=[
                f32(count, ROWS * SUB, LANE),
                f32(count, ROWS * SUB, LANE),
                f32(count, SUB, LANE),
            ],
            scratch_shapes=[
                pltpu.VMEM((rows * SUB, LANE), jnp.float32),
                pltpu.VMEM((rows, LANE), jnp.float32),
            ],
            compiler_params=params(),
            name=f"inner_{p}",
        )(after(mean, token), stored)

    def border(p, sums, token):
        first, count, order = parts[p]
        totals, last, pixel_sum = sums
        kept, sent = pl.pallas_call(
            functools.partial(border_kernel, first - spans[span_of[p]][0]),
            in_specs=[SMEM, SMEM] + [VMEM] * 4,
            out_specs=[VMEM, VMEM],
            out_shape=[
                f32(count, ROWS // 2 * SUB, LANE),
                f32(count, (ROWS // 2 + 1) * SUB, LANE),
            ],
            scratch_shapes=[pltpu.SMEM((EDGE_ROWS,), jnp.float32)],
            compiler_params=params(),
            name=f"border_{p}",
        )(next_mean, sides[order[0]], after(next_edges[span_of[p]], token), last, totals, pixel_sum)
        return Part(order, uppers, kept, sent)

    sums = []
    token = mean
    local = []
    for p in range(len(parts)):
        local.append(inner(p, token))
        token = local[p][2]
    for p in range(len(parts)):
        sums.append(border(p, local[p], token))
        token = sums[p].sent
    while not all(part.finished() for part in sums):
        for part in sums:
            if not part.finished():
                token = part.advance(token)
    out = None
    for p, (first, count, order) in enumerate(parts):
        held = [] if out is None else [out]
        part = sums[p]
        out = pl.pallas_call(
            functools.partial(finish_kernel, first, total_frames),
            in_specs=[SMEM, VMEM, VMEM, VMEM]
            + [pl.BlockSpec(memory_space=pl.ANY)] * len(held),
            out_specs=pl.BlockSpec(memory_space=pl.ANY),
            out_shape=f32(LEVELS, LAGS, pixels),
            scratch_shapes=[
                pltpu.VMEM((count, LEVELS, LAGS, GROUP), jnp.float32),
                pltpu.SemaphoreType.DMA((count,)),
            ],
            input_output_aliases={4: 0} if held else {},
            compiler_params=params(),
            name=f"finish_{p}",
        )(sides[order[0]], part.cur, part.got, part.sums, *held)
    return out


def solution(mesh):
    return jax.shard_map(
        on_device,
        mesh=mesh,
        in_specs=(P("tm", "pix"), P("pix")),
        out_specs=P(None, None, "pix"),
        check_vma=False,
    )
```

```python
import functools

import jax
import jax.numpy as jnp
from jax import lax
from jax.experimental import pallas as pl
from jax.experimental.pallas import tpu as pltpu
from jax.sharding import PartitionSpec as P

LEVELS = 4
LAGS = 16
SUB, LANE = 8, 128
GROUP = SUB * LANE
VMEM_LIMIT = 16 * 1024 * 1024


def tile(ref, row):
    return ref[row * SUB : (row + 1) * SUB, :]


def edge_kernel(first, x_hbm, w_hbm, sums_ref, edge_ref, x_ref, w_ref, tall_ref, acc_ref, sem, w_sem):
    groups, rows, _ = x_ref.shape
    half = LAGS // 2

    def fetch(g):
        at = pl.ds(pl.multiple_of((first + g) * GROUP, GROUP), GROUP)
        return pltpu.make_async_copy(x_hbm.at[:, at], x_ref.at[g], sem.at[g])

    weights = pltpu.make_async_copy(w_hbm, w_ref, w_sem)
    weights.start()
    for g in range(groups):
        fetch(g).start()
    acc_ref[...] = jnp.zeros_like(acc_ref)
    weights.wait()

    def one_group(g, carry):
        fetch(g).wait()
        for c in range(SUB):
            at = pl.ds(pl.multiple_of((first + g) * GROUP + c * LANE, LANE), LANE)
            weight = jnp.broadcast_to(w_ref[:, at], (SUB, LANE))
            acc_ref[rows : rows + SUB, :] += weight
            for i in range(rows // SUB):
                part = slice(i * SUB, (i + 1) * SUB)
                value = x_ref[g, part, c * LANE : (c + 1) * LANE]
                acc_ref[part, :] += value * weight
                tall_ref[pl.ds(i * SUB * SUB + c, SUB, stride=SUB), :] = value
        edge_ref[g, : LAGS * SUB, :] = tall_ref[: LAGS * SUB, :]
        for level in range(1, LEVELS):
            span = 1 << level
            for j in range(half):
                group = [tile(tall_ref, (half + j) * span + s) for s in range(span)]
                while len(group) > 1:
                    group = [(a + b) * 0.5 for a, b in zip(group[::2], group[1::2])]
                row = LAGS + (level - 1) * half + j
                edge_ref[g, row * SUB : (row + 1) * SUB, :] = group[0]
        return carry

    lax.fori_loop(0, groups, one_group, 0)
    sums_ref[...] = jnp.sum(acc_ref[...], axis=1, keepdims=True)


def lag_step(read, near, far, totals):
    window = [read(i) for i in range(LAGS)]
    out = list(totals)
    for i in range(near):
        for k in range(1, LAGS + 1):
            if i + k < far:
                if i + k == len(window):
                    window.append(read(i + k))
                out[k - 1] = out[k - 1] + window[i] * window[i + k]
    return out


def inner_kernel(mean_ref, x_ref, totals_ref, last_ref, sum_ref, series_ref, wide_ref):
    rows = x_ref.shape[0]

    @pl.when(pl.program_id(0) == 0)
    def _():
        for t in range(rows):
            wide_ref[t : t + 1, :] = jnp.full((1, LANE), mean_ref[t], jnp.float32)

    for c in range(SUB):
        total = None
        for i in range(rows // SUB):
            part = slice(i * SUB, (i + 1) * SUB)
            value = x_ref[part, c * LANE : (c + 1) * LANE] + wide_ref[part, :]
            series_ref[pl.ds(i * SUB * SUB + c, SUB, stride=SUB), :] = value
            total = value if total is None else total + value
        sum_ref[0, c : c + 1, :] = jnp.sum(total, axis=0, keepdims=True)
    zero = jnp.zeros((SUB, LANE), jnp.float32)
    for level in range(LEVELS):
        count = rows >> level
        chunks = count // LAGS

        def reader(chunk):
            start = chunk * (LAGS * SUB)

            def read(i):
                return series_ref[pl.ds(pl.multiple_of(start + i * SUB, SUB), SUB), :]

            return read

        def body(chunk, totals):
            return tuple(lag_step(reader(chunk), LAGS, 2 * LAGS, totals))

        totals = tuple([zero] * LAGS)
        if chunks > 1:
            totals = lax.fori_loop(0, chunks - 1, body, totals)
        read = reader(chunks - 1)
        totals = lag_step(read, LAGS, LAGS, totals)
        old = [read(i) for i in range(LAGS)]
        for i in range(LAGS):
            row = level * LAGS + i
            totals_ref[0, row * SUB : (row + 1) * SUB, :] = totals[i]
            last_ref[0, row * SUB : (row + 1) * SUB, :] = old[i]
        if level < LEVELS - 1:
            for i in range(count // 2):
                pair = tile(series_ref, 2 * i) + tile(series_ref, 2 * i + 1)
                series_ref[i * SUB : (i + 1) * SUB, :] = pair * 0.5


def border_kernel(offset, mean_ref, side_ref, edge_ref, last_ref, totals_ref,
                  sum_ref, kept_ref, sent_ref, level_mean_ref):
    half = LAGS // 2
    split = LEVELS // 2
    side = side_ref[0]
    groups = kept_ref.shape[0]
    for j in range(LAGS):
        level_mean_ref[j] = mean_ref[j]
    for level in range(1, LEVELS):
        span = 1 << level
        for j in range(half):
            group = [mean_ref[(half + j) * span + s] for s in range(span)]
            while len(group) > 1:
                group = [(a + b) * 0.5 for a, b in zip(group[::2], group[1::2])]
            level_mean_ref[LAGS + (level - 1) * half + j] = group[0]

    def one_group(slot, carry):
        sent_ref[slot, ROWS // 2 * SUB :, :] = sum_ref[slot]
        new = [
            edge_ref[slot + offset, j * SUB : (j + 1) * SUB, :] + level_mean_ref[j]
            for j in range(LAGS)
        ]
        for level in range(LEVELS):
            if level > 0:
                fresh = [(a + b) * 0.5 for a, b in zip(new[::2], new[1::2])]
                for j in range(half):
                    row = LAGS + (level - 1) * half + j
                    fresh.append(
                        edge_ref[slot + offset, row * SUB : (row + 1) * SUB, :]
                        + level_mean_ref[row]
                    )
                new = fresh
            base = level * LAGS
            old = [
                last_ref[slot, (base + i) * SUB : (base + i + 1) * SUB, :]
                for i in range(LAGS)
            ]
            totals = []
            for k in range(1, LAGS + 1):
                row = base + k - 1
                total = totals_ref[slot, row * SUB : (row + 1) * SUB, :]
                for i in range(LAGS - k, LAGS):
                    total = total + old[i] * new[i + k - LAGS]
                totals.append(total)
            upper, base = level // split, (level % split) * LAGS

            def put(ref, totals=totals, base=base):
                for i, total in enumerate(totals):
                    ref[slot, (base + i) * SUB : (base + i + 1) * SUB, :] = total

            pl.when(side == upper)(functools.partial(put, kept_ref))
            pl.when(side != upper)(functools.partial(put, sent_ref))
        return carry

    lax.fori_loop(0, groups, one_group, 0)


def finish_kernel(first, total_frames, side_ref, mine_ref, got_ref, sum_ref, *refs):
    out_hbm, out_ref, sem = refs[-3:]
    split = LEVELS // 2
    groups = mine_ref.shape[0]
    side = side_ref[0]

    def put(g):
        at = pl.ds((first + g) * GROUP, GROUP)
        return pltpu.make_async_copy(out_ref.at[g], out_hbm.at[:, :, at], sem.at[g])

    for g in range(groups):
        for c in range(SUB):
            mean = sum_ref[g, c : c + 1, :] / total_frames
            square = jnp.broadcast_to(mean * mean, (SUB, LANE))
            for level in range(LEVELS):
                own = side == level // split
                for i in range(LAGS // SUB):
                    lag = lax.broadcasted_iota(jnp.int32, (SUB, LANE), 0) + (i * SUB + 1)
                    count = ((total_frames >> level) - lag).astype(jnp.float32)
                    row = (level % split) * LAGS + i * SUB
                    at = pl.ds(row * SUB + c, SUB, stride=SUB)
                    total = jnp.where(own, mine_ref[g, at, :], got_ref[g, at, :])
                    out_ref[
                        g, level, i * SUB : (i + 1) * SUB, c * LANE : (c + 1) * LANE
                    ] = total / (count * square)
        put(g).start()
    for g in range(groups):
        put(g).wait()


ROWS = LEVELS * LAGS
EDGE_ROWS = LAGS + (LEVELS - 1) * (LAGS // 2)
SMEM = pl.BlockSpec(memory_space=pltpu.SMEM)
VMEM = pl.BlockSpec(memory_space=pltpu.VMEM)


def params():
    return pltpu.CompilerParams(vmem_limit_bytes=VMEM_LIMIT)


def in_hbm(value):
    return pltpu.with_memory_space_constraint(value, pltpu.HBM)


def f32(*shape):
    return jax.ShapeDtypeStruct(shape, jnp.float32)


def by_group(rows):
    return pl.BlockSpec((1, rows * SUB, LANE), lambda g: (g, 0, 0))


def swap(block, masks):
    size, cores = lax.axis_size("tm"), lax.axis_size("pix")
    route = [
        (i * cores + c, (i ^ masks[c % 2]) * cores + c)
        for i in range(size)
        for c in range(cores)
    ]
    return lax.ppermute(block, ("tm", "pix"), route)


def after(value, token):
    return lax.optimization_barrier((value, token))[0]


class Part:
    def __init__(self, order, uppers, kept, sent):
        self.order = order
        self.uppers = uppers
        self.kept, self.sent = kept, sent
        self.sums = sent[:, kept.shape[1] :]
        steps = len(order)
        self.route = list(range(steps)) + list(reversed(range(steps - 1)))
        self.at = 0
        self.got = swap(sent, order[0])

    def finished(self):
        return self.at == len(self.route) - 1

    def advance(self, token):
        steps = len(self.order)
        got = after(self.got, token)
        if self.at < steps:
            rows = self.kept.shape[1]
            self.cur = self.kept + got[:, :rows]
            self.sums = self.sums + got[:, rows:]
        else:
            upper = self.uppers[self.order[self.route[self.at]]]
            low = jnp.where(upper, got, self.cur)
            high = jnp.where(upper, self.cur, got)
            self.cur = jnp.concatenate([low, high], axis=1)
        self.at += 1
        mask = self.order[self.route[self.at]]
        if self.at < steps:
            if self.at == steps - 1:
                self.kept = self.sent = self.cur
            else:
                half = self.cur.shape[1] // 2
                low, high = self.cur[:, :half], self.cur[:, half:]
                self.kept = jnp.where(self.uppers[mask], high, low)
                self.sent = jnp.where(self.uppers[mask], low, high)
            self.sent = jnp.concatenate([self.sent, self.sums], axis=1)
        else:
            self.sent = self.cur
        self.got = swap(self.sent, mask)
        return self.sent


def plan(groups, bits):
    x, y, z = (bits + bits[-1:] * 2)[:3]
    cuts = [groups * i // 8 for i in CUTS]
    even = [[z, y, x], [y, x, z], [x, z, y]]
    odd = [[y, x, z], [x, z, y], [z, y, x]]
    orders = [list(zip(e + bits[3:], o + bits[3:])) for e, o in zip(even, odd)]
    orders = [o[: len(bits)] for o in orders]
    return [(a, b - a, o) for a, b, o in zip(cuts, cuts[1:], orders)]


CUTS = (0, 3, 6, 8)


def on_device(frames, ref_weight):
    rows, pixels = frames.shape
    groups = pixels // GROUP
    size = lax.axis_size("tm")
    total_frames = rows * size
    bits = [1 << b for b in range(size.bit_length() - 1)]
    parts = plan(groups, bits)
    me = lax.axis_index("tm")
    odd = lax.axis_index("pix") % 2 == 1
    uppers = {
        masks: (me & jnp.where(odd, masks[1], masks[0])) != 0
        for _, _, order in parts
        for masks in order
    }
    sides = {o[0]: uppers[o[0]].astype(jnp.int32).reshape(1) for _, _, o in parts}
    ref_weight, uppers, sides = lax.optimization_barrier((ref_weight, uppers, sides))
    stored = in_hbm(frames)
    head = parts[0][1]
    spans = [(0, head), (head, groups - head)]
    back = [(i, i - 1) for i in range(1, size)]
    all_sums, edges = [], []
    for p, (first, count) in enumerate(spans):
        source = stored if p == 0 else in_hbm(after(frames, all_sums[0]))
        sums, edge = pl.pallas_call(
            functools.partial(edge_kernel, first),
            in_specs=[pl.BlockSpec(memory_space=pl.ANY)] * 2,
            out_specs=[VMEM, VMEM],
            out_shape=[f32(rows + SUB, 1), f32(count, EDGE_ROWS * SUB, LANE)],
            scratch_shapes=[
                pltpu.VMEM((count, rows, GROUP), jnp.float32),
                pltpu.VMEM((1, pixels), jnp.float32),
                pltpu.VMEM((rows * SUB, LANE), jnp.float32),
                pltpu.VMEM((rows + SUB, LANE), jnp.float32),
                pltpu.SemaphoreType.DMA((count,)),
                pltpu.SemaphoreType.DMA,
            ],
            compiler_params=params(),
            name=f"edges_{p}",
        )(source, in_hbm(ref_weight.reshape(1, pixels)))
        all_sums.append(sums)
        edges.append(edge)
    sums = sum(all_sums[1:], all_sums[0])
    next_edges = [lax.ppermute(edges[0], "tm", back)]
    sums = lax.psum(sums[:, 0], "pix")
    mean = sums[:rows] / sums[rows]
    next_mean = lax.ppermute(mean, "tm", back)
    for edge in edges[1:]:
        next_edges.append(lax.ppermute(after(edge, mean), "tm", back))

    def inner(p, token):
        first, count, _ = parts[p]
        return pl.pallas_call(
            inner_kernel,
            grid=(count,),
            in_specs=[
                SMEM,
                pl.BlockSpec((rows, GROUP), lambda g: (0, g + first)),
            ],
            out_specs=[by_group(ROWS), by_group(ROWS), by_group(1)],
            out_shape=[
                f32(count, ROWS * SUB, LANE),
                f32(count, ROWS * SUB, LANE),
                f32(count, SUB, LANE),
            ],
            scratch_shapes=[
                pltpu.VMEM((rows * SUB, LANE), jnp.float32),
                pltpu.VMEM((rows, LANE), jnp.float32),
            ],
            compiler_params=params(),
            name=f"inner_{p}",
        )(after(mean, token), stored)

    def border(p, sums, token):
        first, count, order = parts[p]
        totals, last, pixel_sum = sums
        kept, sent = pl.pallas_call(
            functools.partial(border_kernel, first - spans[p > 0][0]),
            in_specs=[SMEM, SMEM] + [VMEM] * 4,
            out_specs=[VMEM, VMEM],
            out_shape=[
                f32(count, ROWS // 2 * SUB, LANE),
                f32(count, (ROWS // 2 + 1) * SUB, LANE),
            ],
            scratch_shapes=[pltpu.SMEM((EDGE_ROWS,), jnp.float32)],
            compiler_params=params(),
            name=f"border_{p}",
        )(next_mean, sides[order[0]], after(next_edges[p > 0], token), last, totals, pixel_sum)
        return Part(order, uppers, kept, sent)

    sums = []
    token = mean
    local = []
    for p in range(len(parts)):
        local.append(inner(p, token))
        token = local[p][2]
    for p in range(len(parts)):
        sums.append(border(p, local[p], token))
        token = sums[p].sent
    while not all(part.finished() for part in sums):
        for part in sums:
            if not part.finished():
                token = part.advance(token)
    out = None
    for p, (first, count, order) in enumerate(parts):
        held = [] if out is None else [out]
        part = sums[p]
        out = pl.pallas_call(
            functools.partial(finish_kernel, first, total_frames),
            in_specs=[SMEM, VMEM, VMEM, VMEM]
            + [pl.BlockSpec(memory_space=pl.ANY)] * len(held),
            out_specs=pl.BlockSpec(memory_space=pl.ANY),
            out_shape=f32(LEVELS, LAGS, pixels),
            scratch_shapes=[
                pltpu.VMEM((count, LEVELS, LAGS, GROUP), jnp.float32),
                pltpu.SemaphoreType.DMA((count,)),
            ],
            input_output_aliases={4: 0} if held else {},
            compiler_params=params(),
            name=f"finish_{p}",
        )(sides[order[0]], part.cur, part.got, part.sums, *held)
    return out


def solution(mesh):
    return jax.shard_map(
        on_device,
        mesh=mesh,
        in_specs=(P("tm", "pix"), P("pix")),
        out_specs=P(None, None, "pix"),
        check_vma=False,
    )
```
